32 devices in a mesh: groups: 2 (over y), psg: 16 (over z, x, core).
Axes of the slice: x: 2, y: 2, z: 4, core: 2. Of those that a mesh axis runs over, the one named last changes fastest.
Arguments:
- tail_hidden_states: bfloat16 [256, 8192], P('groups', 'psg'), parts along dimension 0, may hold values from -6 to 6
- passage_hidden_states: bfloat16 [2048, 8192], P(('groups', 'psg')), parts along dimension 0, may hold values from -6 to 6
- lengths: int32 [4], P('groups'), parts along dimension 0, may hold values from 1 to 768, 1024 in all
- storage_order: int32 [4], P('groups'), parts along dimension 0, may hold values from 0 to 1, each once
- orders: int32 [6, 2], P('groups'), parts along dimension 0, may hold values from 0 to 1, each once within a row
- w_query: bfloat16 [8192, 4096], P('psg'), may hold values from -1 to 1
- key_weight: bfloat16 [8192, 512], P('psg'), may hold values from -0.0625 to 0.0625
- value_weight: bfloat16 [8192, 512], P('psg'), may hold values from -0.0625 to 0.0625
- w_out: bfloat16 [4096, 8192], P(None, 'psg'), may hold values from -0.09375 to 0.09375
- norm_gain: float32 [8192], P('psg'), may hold values from 0.1 to 1.9
Outputs:
- layer_out: bfloat16 [256, 8192], P('groups', 'psg'), parts along dimension 0
The draws below stay inside these ranges and needn't reach their ends.
There are 2 independent parts, one for each index of `groups`. The reference program is written for one: setup_inputs(seed, part) draws one part's arguments, and reference() takes and returns one part's arrays. A program takes and returns all parts, laid end to end along the dimension named above; an argument that names none is the same for every part. Nothing has to cross between parts.
Inputs may be any that keep to these rules, and one draw needn't show every extreme that they name: `lengths`: they sum to 1024; the largest is 768. `storage_order`: A permutation of the passages. `orders`: each row is a permutation of the passages.
All inputs are finite; a program needn't handle non-finite values.
Results may differ from the reference program's by a relative error of at most 0.01065.
The reference program's roundings to bfloat16 on the way count: a program that leaves them out, or rounds other values in their place, can miss the bound.
Values may be sent and summed in bfloat16 or wider, within the bound.
No kernel may reach another device: no remote copies, remote signals or barrier semaphores. Data moves between devices by JAX's collectives and lax.ppermute only.
A program may use at most 128 MiB of HBM per device.

```python
import math
import jax
import jax.numpy as jnp
import numpy as np
from jax import lax

MODEL_WIDTH = 8192
QUERY_HEAD_COUNT = 32
KEY_VALUE_HEADS = 4
HEAD_SIZE = 128
TAIL_TOKENS = 128
PERMS = 3
LMAX = 768
PASSAGE_TOKENS = 1024
PASSAGES = 2


def draw_w_query(key, part):
    entry_key = jax.random.fold_in(key, 11)
    level_key = jax.random.fold_in(key, 12)
    order_key = jax.random.fold_in(key, 13)
    entries = jax.random.truncated_normal(entry_key, -6.0, 6.0, (MODEL_WIDTH, QUERY_HEAD_COUNT * HEAD_SIZE), jnp.float32)
    sharpest = 24.0
    ranks = jax.random.permutation(order_key, QUERY_HEAD_COUNT).astype(jnp.float32)
    jitter = jax.random.uniform(level_key, (QUERY_HEAD_COUNT,), jnp.float32)
    head_scale = jnp.exp((ranks + jitter) / QUERY_HEAD_COUNT * math.log(sharpest))
    column_scale = jnp.repeat(head_scale, HEAD_SIZE)
    scaled = entries * column_scale[None, :] / math.sqrt(MODEL_WIDTH)
    return jnp.clip(scaled, -1.0, 1.0).astype(jnp.bfloat16)


def shard_levels(stream_key, extent, shards, low, largest):
    def one(position, parts):
        steps = jax.random.uniform(jax.random.fold_in(jax.random.fold_in(stream_key, 6), position), (parts,), jnp.float32, low / len(shards), largest / len(shards))
        return jnp.repeat(jnp.exp(steps), extent[position] // parts).reshape((-1,) + (1,) * (len(extent) - position - 1))

    loudness = one(*shards[0])
    for cut in shards[1:]:
        loudness = loudness * one(*cut)
    return loudness


def split_up(number_of, total, most, skew):
    weights = [(1 << 20) // math.isqrt(grade ** skew) + 1 for grade in range(2, number_of + 1)]
    rest, given = total - most - (number_of - 1), [1] * (number_of - 1)
    while rest > 0:
        free = [i for i in range(number_of - 1) if given[i] < most]
        pool, budget = sum([weights[i] for i in free]), rest
        for i in free:
            addition = min(most - given[i], max(1, budget * weights[i] // pool), rest)
            given[i] = given[i] + addition
            rest = rest - addition
    return np.array([most] + given)


def ragged_sizes(own_key, amount, total, limit, skew):
    if amount == 2:
        one = jax.random.randint(own_key, (), max(1, total - limit), min(limit, total - 1) + 1)
        return jnp.stack([one, total - one])
    sizes = jnp.asarray(split_up(amount, total, limit, skew), jnp.int32)
    couples = (amount - 1) // 2
    donor, taker = sizes[1:1 + 2 * couples:2], sizes[2:2 + 2 * couples:2]
    slack = jnp.minimum(donor - 1, limit - taker)
    passed = jax.random.randint(jax.random.fold_in(own_key, 1), (couples,), 0, 1 << 20) % (slack + 1)
    sizes = sizes.at[1:1 + 2 * couples:2].set(donor - passed).at[2:2 + 2 * couples:2].set(taker + passed)
    return sizes[jax.random.permutation(jax.random.fold_in(own_key, 2), amount)]


def gaussian(key, extent, scale, reach, split=(), kind=jnp.bfloat16):
    result = jax.random.normal(key, extent, jnp.float32) * scale
    if len(split) > 0:
        result = shard_levels(key, extent, split, -0.22, 0.18) * result
    return jnp.clip(result, min=-reach, max=reach).astype(kind)


def setup_inputs(seed: int = 0, part: int = 0) -> dict:
    streams_of = jax.random.split(jax.random.key(seed), 11)
    part_keys = jax.random.split(jax.random.fold_in(streams_of[10], part), 11)
    return {
        "tail_hidden_states": gaussian(part_keys[0], (TAIL_TOKENS, MODEL_WIDTH), 1.0, 6.0, ((1, 16),)),
        "passage_hidden_states": gaussian(part_keys[1], (PASSAGE_TOKENS, MODEL_WIDTH), 1.0, 6.0, ((0, 16),)),
        "lengths": ragged_sizes(part_keys[2], PASSAGES, PASSAGE_TOKENS, LMAX, 2).astype(jnp.int32),
        "storage_order": jax.random.permutation(part_keys[3], PASSAGES).astype(jnp.int32),
        "orders": jax.vmap(lambda own: jax.random.permutation(own, PASSAGES))(jax.random.split(part_keys[4], PERMS)).reshape((PERMS, PASSAGES)).astype(jnp.int32),
        "w_query": draw_w_query(jax.random.fold_in(streams_of[10], 71), part),
        "key_weight": gaussian(streams_of[6], (MODEL_WIDTH, KEY_VALUE_HEADS * HEAD_SIZE), MODEL_WIDTH ** -0.5, 0.0625, ((0, 16),)),
        "value_weight": gaussian(streams_of[7], (MODEL_WIDTH, KEY_VALUE_HEADS * HEAD_SIZE), MODEL_WIDTH ** -0.5, 0.0625, ((0, 16),)),
        "w_out": gaussian(streams_of[8], (QUERY_HEAD_COUNT * HEAD_SIZE, MODEL_WIDTH), (QUERY_HEAD_COUNT * HEAD_SIZE) ** -0.5, 0.09375, ((1, 16),)),
        "norm_gain": jnp.clip(1.0 + 0.18 * jax.random.normal(streams_of[9], (MODEL_WIDTH,), jnp.float32), 0.1, 1.9),
    }


theta_base = 500000.0
epsilon = 1e-05

def rotate(vectors, places):
    half = vectors.shape[-1] // 2
    freqs = theta_base ** (-jnp.arange(half, dtype=jnp.float32) * 2.0 / vectors.shape[-1])
    angles = places.astype(jnp.float32)[:, None] * freqs[None, :]
    cosine = jnp.cos(angles)[:, None, :]
    sine = jnp.sin(angles)[:, None, :]
    first = vectors[..., :half]
    second = vectors[..., half:]
    return jnp.concatenate([first * cosine - second * sine, second * cosine + first * sine], axis=-1)

def key_positions(lengths, storage_order, orders):
    passages = lengths.shape[0]
    stored_lengths = lengths[storage_order]
    ends = jnp.cumsum(stored_lengths).astype(jnp.int32)
    starts = (ends - stored_lengths).astype(jnp.int32)
    row_ids = jnp.arange(PASSAGE_TOKENS, dtype=jnp.int32)
    slots = lax.optimization_barrier(jnp.sum((ends[None, :] <= row_ids[:, None]).astype(jnp.int32), axis=1))
    passage_of = storage_order[slots]
    offsets = row_ids - starts[slots]
    ordered = lengths[orders]
    order_starts = (jnp.cumsum(ordered, axis=1) - ordered).astype(jnp.int32)
    order_ids = jnp.arange(orders.shape[0], dtype=jnp.int32)[:, None]
    placed = jnp.zeros((orders.shape[0], passages), jnp.int32).at[order_ids, orders].set(order_starts)
    return placed[:, passage_of] + offsets[None, :]

def reference(tail_hidden_states, passage_hidden_states, lengths, storage_order, orders, w_query, key_weight, value_weight, w_out, norm_gain):
    query_group = QUERY_HEAD_COUNT // KEY_VALUE_HEADS
    tail_pos = PASSAGE_TOKENS + jnp.arange(TAIL_TOKENS, dtype=jnp.int32)
    query_vectors = jnp.dot(tail_hidden_states, w_query, preferred_element_type=jnp.float32).reshape(TAIL_TOKENS, QUERY_HEAD_COUNT, HEAD_SIZE)
    query_vectors = rotate(query_vectors, tail_pos).astype(jnp.bfloat16)
    query_vectors = lax.optimization_barrier(query_vectors).astype(jnp.float32).reshape(TAIL_TOKENS, KEY_VALUE_HEADS, query_group, HEAD_SIZE)
    tail_key_rows = jnp.dot(tail_hidden_states, key_weight, preferred_element_type=jnp.float32).reshape(TAIL_TOKENS, KEY_VALUE_HEADS, HEAD_SIZE)
    tail_key_rows = lax.optimization_barrier(rotate(tail_key_rows, tail_pos).astype(jnp.bfloat16)).astype(jnp.float32)
    tail_value_rows = jnp.dot(tail_hidden_states, value_weight, preferred_element_type=jnp.float32).astype(jnp.bfloat16)
    tail_value_rows = lax.optimization_barrier(tail_value_rows).astype(jnp.float32).reshape(TAIL_TOKENS, KEY_VALUE_HEADS, HEAD_SIZE)
    unrotated_key = jnp.dot(passage_hidden_states, key_weight, preferred_element_type=jnp.float32).reshape(PASSAGE_TOKENS, KEY_VALUE_HEADS, HEAD_SIZE)
    passage_values = jnp.dot(passage_hidden_states, value_weight, preferred_element_type=jnp.float32).astype(jnp.bfloat16)
    passage_values = lax.optimization_barrier(passage_values).astype(jnp.float32).reshape(PASSAGE_TOKENS, KEY_VALUE_HEADS, HEAD_SIZE)
    token_positions = key_positions(lengths, storage_order, orders)
    scale = HEAD_SIZE ** (-0.5)
    tail_scores = jnp.einsum('tkgd,skd->tkgs', query_vectors, tail_key_rows) * scale
    causal = jnp.arange(TAIL_TOKENS)[None, :] <= jnp.arange(TAIL_TOKENS)[:, None]
    tail_scores = jnp.where(causal[:, None, None, :], tail_scores, -1e+30)

    def single_ordering(running, places):
        keys = lax.optimization_barrier(rotate(unrotated_key, places).astype(jnp.bfloat16)).astype(jnp.float32)
        scores = jnp.einsum('tkgd,nkd->tkgn', query_vectors, keys) * scale
        peak = jnp.maximum(lax.optimization_barrier(jnp.max(scores, axis=-1)), lax.optimization_barrier(jnp.max(tail_scores, axis=-1)))[..., None]
        weights = jnp.exp(scores - peak)
        tail_weights = jnp.exp(tail_scores - peak)
        denom = lax.optimization_barrier(jnp.sum(weights, axis=-1)) + lax.optimization_barrier(jnp.sum(tail_weights, axis=-1))
        weights_b = lax.optimization_barrier(weights.astype(jnp.bfloat16)).astype(jnp.float32)
        tail_b = lax.optimization_barrier(tail_weights.astype(jnp.bfloat16)).astype(jnp.float32)
        numer = jnp.einsum('tkgn,nkd->tkgd', weights_b, passage_values) + jnp.einsum('tkgs,skd->tkgd', tail_b, tail_value_rows)
        return (running + numer / denom[..., None], None)
    agreed_output, unused_slot = lax.scan(single_ordering, jnp.zeros((TAIL_TOKENS, KEY_VALUE_HEADS, query_group, HEAD_SIZE), jnp.float32), token_positions)
    mixed = agreed_output.reshape(TAIL_TOKENS, QUERY_HEAD_COUNT * HEAD_SIZE).astype(jnp.bfloat16)
    projected = jnp.dot(mixed, w_out, preferred_element_type=jnp.float32)
    factor = lax.rsqrt(lax.optimization_barrier(jnp.mean(projected * projected, axis=1, keepdims=True)) + epsilon)
    return (projected * factor * norm_gain[None, :]).astype(jnp.bfloat16)
```

```python
import functools

import jax
import jax.numpy as jnp
from jax import lax
from jax.experimental import pallas as pl
from jax.experimental.pallas import tpu as pltpu
from jax.sharding import PartitionSpec as P

MODEL_WIDTH = 8192
HEAD_SIZE = 128


theta_base = 500000.0
epsilon = 1e-05


def joined(part, axis, combine):
    gathered = jax.tree.map(lambda a: lax.all_gather(a, axis), part)

    def take(source):
        return jax.tree.map(lambda a: lax.dynamic_index_in_dim(a, source, 0, False), gathered)

    return lax.fori_loop(
        1, lax.axis_size(axis), lambda source, state: combine(state, take(source)), take(0)
    )


def rotate(vectors, places):
    half = vectors.shape[-1] // 2
    freqs = theta_base ** (-jnp.arange(half, dtype=jnp.float32) * 2.0 / vectors.shape[-1])
    angles = places.astype(jnp.float32)[:, None] * freqs[None, :]
    cosine = jnp.cos(angles)[:, None, :]
    sine = jnp.sin(angles)[:, None, :]
    first = vectors[..., :half]
    second = vectors[..., half:]
    return jnp.concatenate(
        [first * cosine - second * sine, second * cosine + first * sine], axis=-1
    )


def general_device(
    tail_hidden_states,
    passage_hidden_states,
    lengths,
    storage_order,
    orders,
    w_query,
    key_weight,
    value_weight,
    w_out,
    norm_gain,
):
    shards = lax.axis_size("psg")
    device = lax.axis_index("psg")
    row_count = passage_hidden_states.shape[0]
    tail_count = tail_hidden_states.shape[0]
    kv_heads = key_weight.shape[1] // HEAD_SIZE
    query_heads = w_query.shape[1] // HEAD_SIZE
    query_group = query_heads // kv_heads
    total_keys = row_count * shards
    query_part = jnp.dot(tail_hidden_states, w_query, preferred_element_type=jnp.float32)
    key_part = jnp.dot(tail_hidden_states, key_weight, preferred_element_type=jnp.float32)
    value_part = jnp.dot(tail_hidden_states, value_weight, preferred_element_type=jnp.float32)
    query_sum, key_sum, value_sum = lax.psum((query_part, key_part, value_part), "psg")
    tail_pos = total_keys + jnp.arange(tail_count, dtype=jnp.int32)
    query_vectors = rotate(query_sum.reshape(tail_count, query_heads, HEAD_SIZE), tail_pos).astype(
        jnp.bfloat16
    )
    query_vectors = query_vectors.reshape(tail_count, kv_heads, query_group, HEAD_SIZE)
    tail_key_rows = rotate(key_sum.reshape(tail_count, kv_heads, HEAD_SIZE), tail_pos).astype(
        jnp.bfloat16
    )
    tail_value_rows = value_sum.astype(jnp.bfloat16).reshape(tail_count, kv_heads, HEAD_SIZE)

    def add_block(piece):
        return jnp.dot(passage_hidden_states, piece, preferred_element_type=jnp.float32)

    unrotated_key = add_block(lax.all_gather(key_weight, "psg", axis=0, tiled=True))
    raw_value = add_block(lax.all_gather(value_weight, "psg", axis=0, tiled=True))
    numbers = jnp.arange(lengths.shape[0], dtype=jnp.int32)
    pick = (storage_order[:, None] == numbers[None, :]).astype(jnp.int32)
    stored_lengths = jnp.sum(pick * lengths[None, :], axis=1)
    ends = jnp.cumsum(stored_lengths)
    starts = ends - stored_lengths
    row_ids = device * row_count + jnp.arange(row_count, dtype=jnp.int32)
    slots = jnp.sum((ends[None, :] <= row_ids[:, None]).astype(jnp.int32), axis=1)
    in_slot = (slots[:, None] == numbers[None, :]).astype(jnp.int32)
    offsets = row_ids - jnp.sum(in_slot * starts[None, :], axis=1)
    passage_hot = jnp.dot(in_slot, pick)
    ordered_hot = (orders[:, :, None] == numbers[None, None, :]).astype(jnp.int32)
    ordered_lengths = jnp.sum(ordered_hot * lengths[None, None, :], axis=2)
    order_starts = jnp.cumsum(ordered_lengths, axis=1) - ordered_lengths
    placed = jnp.sum(ordered_hot * order_starts[:, :, None], axis=1)
    token_positions = (
        jnp.sum(passage_hot[None, :, :] * placed[:, None, :], axis=2) + offsets[None, :]
    )
    passage_values = raw_value.astype(jnp.bfloat16).reshape(row_count, kv_heads, HEAD_SIZE)
    unrotated_key = unrotated_key.reshape(row_count, kv_heads, HEAD_SIZE)
    scale = HEAD_SIZE ** (-0.5)
    tail_scores = (
        jnp.einsum(
            "tkgd,skd->tkgs", query_vectors, tail_key_rows, preferred_element_type=jnp.float32
        )
        * scale
    )
    causal = jnp.arange(tail_count)[None, :] <= jnp.arange(tail_count)[:, None]
    tail_scores = jnp.where(causal[:, None, None, :], tail_scores, -1e30)
    tail_top = jnp.max(tail_scores, axis=-1)

    def scores_for(places):
        keys = rotate(unrotated_key, places).astype(jnp.bfloat16)
        return (
            jnp.einsum("tkgd,nkd->tkgn", query_vectors, keys, preferred_element_type=jnp.float32)
            * scale
        )

    def local_stats(places):
        scores = scores_for(places)
        peak = jnp.maximum(jnp.max(scores, axis=-1), tail_top)
        return (peak, jnp.sum(jnp.exp(scores - peak[..., None]), axis=-1))

    def combine(first, second):
        peak = jnp.maximum(first[0], second[0])
        return (peak, first[1] * jnp.exp(first[0] - peak) + second[1] * jnp.exp(second[0] - peak))

    peaks, totals = joined(lax.map(local_stats, token_positions), "psg", combine)

    def accumulate(running, inputs):
        places, peak, partial_value = inputs
        weights = jnp.exp(scores_for(places) - peak[..., None])
        tail_weights = jnp.exp(tail_scores - peak[..., None])
        denom = (partial_value + jnp.sum(tail_weights, axis=-1))[..., None]
        shared = jnp.einsum(
            "tkgn,nkd->tkgd",
            weights.astype(jnp.bfloat16),
            passage_values,
            preferred_element_type=jnp.float32,
        )
        own = jnp.einsum(
            "tkgs,skd->tkgd",
            tail_weights.astype(jnp.bfloat16),
            tail_value_rows,
            preferred_element_type=jnp.float32,
        )
        return ((running[0] + shared / denom, running[1] + own / denom), None)

    start_sums = jnp.zeros((tail_count, kv_heads, query_group, HEAD_SIZE), jnp.float32)
    (shared_sum, own_sum), unused_slot = lax.scan(
        accumulate, (start_sums, start_sums), (token_positions, peaks, totals)
    )
    agreed_output = lax.psum(shared_sum, "psg") + own_sum
    mixed = agreed_output.reshape(tail_count, -1).astype(jnp.bfloat16)
    projected = jnp.dot(mixed, w_out, preferred_element_type=jnp.float32)
    squares = lax.psum(jnp.sum(projected * projected, axis=1), "psg")
    factor = lax.rsqrt(squares / MODEL_WIDTH + epsilon)[:, None]
    return (projected * factor * norm_gain[None, :]).astype(jnp.bfloat16)


WIRE = jnp.float16
ROWS_COLUMNS = (((1,), (1,)), ((), ()))


def in_vmem(count):
    return [pl.BlockSpec(memory_space=pltpu.VMEM)] * count


def positions_of(row_ids, lengths, storage_order, orders):
    numbers = jnp.arange(lengths.shape[0], dtype=jnp.int32)
    pick = (storage_order[:, None] == numbers[None, :]).astype(jnp.int32)
    stored_lengths = jnp.sum(pick * lengths[None, :], axis=1)
    ends = jnp.cumsum(stored_lengths)
    starts = ends - stored_lengths
    slots = jnp.sum((ends[None, :] <= row_ids[:, None]).astype(jnp.int32), axis=1)
    in_slot = (slots[:, None] == numbers[None, :]).astype(jnp.int32)
    offsets = row_ids - jnp.sum(in_slot * starts[None, :], axis=1)
    passage_hot = jnp.sum(in_slot[:, :, None] * pick[None, :, :], axis=1)
    ordered_hot = (orders[:, :, None] == numbers[None, None, :]).astype(jnp.int32)
    ordered_lengths = jnp.sum(ordered_hot * lengths[None, None, :], axis=2)
    order_starts = jnp.cumsum(ordered_lengths, axis=1) - ordered_lengths
    placed = jnp.sum(ordered_hot * order_starts[:, :, None], axis=1)
    return jnp.sum(passage_hot[None, :, :] * placed[:, None, :], axis=2) + offsets[None, :]


def turn_tables(places):
    half = HEAD_SIZE // 2
    freqs = theta_base ** (-jnp.arange(half, dtype=jnp.float32) * 2.0 / HEAD_SIZE)
    angles = places.astype(jnp.float32)[:, None] * jnp.tile(freqs, 2)[None, :]
    sign = jnp.where(jnp.arange(HEAD_SIZE) < half, -1.0, 1.0).astype(jnp.float32)
    return jnp.cos(angles), jnp.sin(angles) * sign[None, :]


def turned(vectors, cosine, sine):
    return vectors * cosine + pltpu.roll(vectors, HEAD_SIZE // 2, 1) * sine


def bit_order(count):
    width = count.bit_length() - 1
    return [int(format(s, "b").zfill(width)[::-1], 2) if width else 0 for s in range(count)]


def query_kernel(ring, heads, pos, x_ref, w_ref, keep_ref, send_ref, acc_ref):
    acc_ref[...] = jnp.dot(x_ref[...], w_ref[...], preferred_element_type=jnp.float32)
    tokens = x_ref.shape[0]
    for slot, kb in enumerate(bit_order(ring)):
        unit = pos[1] ^ kb
        out = keep_ref if slot < ring // 2 else send_ref
        for j in range(heads):
            column = pl.multiple_of((unit * heads + j) * HEAD_SIZE, HEAD_SIZE)
            out[slot % (ring // 2), 0, j * tokens : (j + 1) * tokens, :] = acc_ref[
                :, pl.ds(column, HEAD_SIZE)
            ]


def project_kernel(teams, ring, pos, *refs):
    x_refs, t_refs, w_refs = refs[:teams], refs[teams : teams + ring], refs[teams + ring : teams + 2 * ring]
    out_ref, all_ref, acc_ref = refs[teams + 2 * ring :]
    rows, width, mine = x_refs[0].shape[0], t_refs[0].shape[1], t_refs[0].shape[0] // ring
    for kb in range(ring):
        column = pl.multiple_of((pos[1] ^ kb) * width, width)
        place = slice(kb * width, (kb + 1) * width)
        for ka in range(teams):
            first = pl.multiple_of((pos[0] ^ ka) * rows, rows)
            all_ref[pl.ds(first, rows), place] = x_refs[ka][:, pl.ds(column, width)]
        first = pl.multiple_of(pos[1] * mine, mine)
        all_ref[teams * rows :, place] = t_refs[kb][pl.ds(first, mine), :]
    total = None
    for kb in range(ring):
        part = jnp.dot(
            all_ref[:, kb * width : (kb + 1) * width],
            w_refs[kb][...],
            preferred_element_type=jnp.float32,
        )
        total = part if total is None else total + part
    acc_ref[...] = total
    for ka in range(teams):
        column = pl.multiple_of((pos[0] ^ ka) * HEAD_SIZE, HEAD_SIZE)
        out_ref[ka] = acc_ref[:, pl.ds(column, HEAD_SIZE)].astype(out_ref.dtype)


def pack_kernel(perms, k_ref, v_ref, cos_ref, sin_ref, out_ref):
    rows = (out_ref.shape[0] - 2 * k_ref.shape[0]) // (perms - 1)
    mine = k_ref.shape[0] - rows
    for r in range(perms):
        place = slice(r * rows, (r + 1) * rows)
        out_ref[place, :] = turned(k_ref[:rows, :], cos_ref[place, :], sin_ref[place, :]).astype(
            out_ref.dtype
        )
    base = perms * rows
    out_ref[base : base + rows, :] = v_ref[:rows, :]
    out_ref[base + rows : base + rows + mine, :] = turned(
        k_ref[rows:, :], cos_ref[base:, :], sin_ref[base:, :]
    ).astype(out_ref.dtype)
    out_ref[base + rows + mine :, :] = v_ref[rows:, :]


def attend_kernel(perms, ring, rows, tokens, pos, q_ref, cos_ref, sin_ref, *refs):
    g_refs = refs[:ring]
    out_ref, tk_ref, tv_ref, score_ref = refs[ring:]
    mine = tokens // ring
    base = perms * rows
    scale = HEAD_SIZE ** (-0.5)
    query = turned(q_ref[...], cos_ref[...], sin_ref[...]).astype(jnp.bfloat16)
    for kb in range(ring):
        first = pl.multiple_of((pos[1] ^ kb) * mine, mine)
        tk_ref[pl.ds(first, mine), :] = g_refs[kb][base + rows : base + rows + mine, :]
        tv_ref[pl.ds(first, mine), :] = g_refs[kb][base + rows + mine :, :]
    count = q_ref.shape[0]
    tail = (
        lax.dot_general(query, tk_ref[...], ROWS_COLUMNS, preferred_element_type=jnp.float32) * scale
    )
    token = lax.broadcasted_iota(jnp.int32, (count, tokens), 0) & (tokens - 1)
    tail = jnp.where(lax.broadcasted_iota(jnp.int32, (count, tokens), 1) <= token, tail, -1e30)
    tail_top = jnp.max(tail, axis=1, keepdims=True)
    agreed = None
    for r in range(perms):
        top = tail_top
        for kb in range(ring):
            part = (
                lax.dot_general(
                    query,
                    g_refs[kb][r * rows : (r + 1) * rows, :],
                    ROWS_COLUMNS,
                    preferred_element_type=jnp.float32,
                )
                * scale
            )
            score_ref[:, kb * rows : (kb + 1) * rows] = part
            top = jnp.maximum(top, jnp.max(part, axis=1, keepdims=True))
        weights = jnp.exp(tail - top)
        denom = jnp.sum(weights, axis=1, keepdims=True)
        mixed = jnp.dot(
            weights.astype(jnp.bfloat16), tv_ref[...], preferred_element_type=jnp.float32
        )
        for kb in range(ring):
            weights = jnp.exp(score_ref[:, kb * rows : (kb + 1) * rows] - top)
            denom = denom + jnp.sum(weights, axis=1, keepdims=True)
            mixed = mixed + jnp.dot(
                weights.astype(jnp.bfloat16),
                g_refs[kb][base : base + rows, :],
                preferred_element_type=jnp.float32,
            )
        mixed = mixed / denom
        agreed = mixed if agreed is None else agreed + mixed
    out_ref[...] = agreed.astype(out_ref.dtype)


def output_kernel(teams, ring, tokens, pos, *refs):
    y_refs, (w_ref, out_ref, square_ref) = refs[:ring], refs[ring:]
    heads = y_refs[0].shape[1] // tokens
    total = None
    for kb in range(ring):
        for ka in range(teams):
            unit = (pos[0] ^ ka) * ring + (pos[1] ^ kb)
            first = pl.multiple_of(unit * heads * HEAD_SIZE, HEAD_SIZE)
            left = jnp.concatenate(
                [y_refs[kb][ka, j * tokens : (j + 1) * tokens, :] for j in range(heads)], axis=1
            )
            part = jnp.dot(
                left, w_ref[pl.ds(first, heads * HEAD_SIZE), :], preferred_element_type=jnp.float32
            )
            total = part if total is None else total + part
    out_ref[...] = total
    square_ref[...] = lax.dot_general(
        jnp.ones((8, total.shape[1]), jnp.float32),
        total * total,
        ROWS_COLUMNS,
        precision=lax.Precision.HIGHEST,
        preferred_element_type=jnp.float32,
    )


def split_device(
    tail_hidden_states,
    passage_hidden_states,
    lengths,
    storage_order,
    orders,
    w_query,
    key_weight,
    value_weight,
    w_out,
    norm_gain,
):
    shards = lax.axis_size("psg")
    device = lax.axis_index("psg")
    teams = key_weight.shape[1] // HEAD_SIZE
    ring = shards // teams
    tokens, width = tail_hidden_states.shape
    rows = passage_hidden_states.shape[0]
    mine = tokens // ring
    team, seat = device // ring, device % ring
    perms = orders.shape[0]
    heads = w_query.shape[1] // (HEAD_SIZE * shards)
    total_keys = rows * shards
    block = width * ring
    pos = jnp.stack([team, seat]).astype(jnp.int32)

    def swap(x, k):
        return lax.ppermute(x, "psg", [(i, i ^ k) for i in range(shards)])

    def gathered(x):
        pieces, bit = {0: x}, ring // 2
        while bit:
            pieces.update({kb | bit: swap(piece, bit) for kb, piece in list(pieces.items())})
            bit //= 2
        return [pieces[kb] for kb in range(ring)]

    def chunk(ka):
        return lax.dynamic_slice_in_dim(passage_hidden_states, (team ^ ka) * block, block, 1)

    tails = gathered(tail_hidden_states)
    others = [swap(chunk(ka), ka * ring) for ka in range(1, teams)]
    keys_w = gathered(key_weight)
    values_w = gathered(value_weight)

    units = w_query.shape[1] // teams
    part_shape = jax.ShapeDtypeStruct((ring // 2, teams, heads * tokens, HEAD_SIZE), jnp.float32)
    part_spec = pl.BlockSpec((ring // 2, 1, heads * tokens, HEAD_SIZE), lambda i, pos: (0, i, 0, 0))
    keep, send = pl.pallas_call(
        functools.partial(query_kernel, ring, heads),
        name="query_parts",
        grid_spec=pltpu.PrefetchScalarGridSpec(
            num_scalar_prefetch=1,
            grid=(teams,),
            in_specs=[
                pl.BlockSpec((tokens, width), lambda i, pos: (0, 0)),
                pl.BlockSpec((width, units), lambda i, pos: (0, pos[0] ^ i)),
            ],
            out_specs=[part_spec, part_spec],
            scratch_shapes=[pltpu.VMEM((tokens, units), jnp.float32)],
        ),
        out_shape=[part_shape, part_shape],
        cost_estimate=pl.CostEstimate(
            flops=2 * tokens * width * units * teams,
            bytes_accessed=2 * width * units * teams,
            transcendentals=0,
        ),
    )(pos, tail_hidden_states, w_query)
    bit = 1
    while True:
        query_part = keep + swap(send, bit).astype(jnp.float32)
        bit *= 2
        if bit == ring:
            break
        half = query_part.shape[0] // 2
        keep, send = query_part[:half], query_part[half:].astype(WIRE)
    query_part = query_part[0]
    query = query_part[0]
    for ka in range(1, teams):
        query = query + swap(query_part[ka].astype(WIRE), ka * ring).astype(jnp.float32)

    def project(weights, name):
        count = teams * rows + mine
        return pl.pallas_call(
            functools.partial(project_kernel, teams, ring),
            name=name,
            grid_spec=pltpu.PrefetchScalarGridSpec(
                num_scalar_prefetch=1,
                grid=(1,),
                in_specs=[pl.BlockSpec((rows, block), lambda i, pos: (0, pos[0]))]
                + in_vmem(teams - 1 + 2 * ring),
                out_specs=pl.BlockSpec(memory_space=pltpu.VMEM),
                scratch_shapes=[
                    pltpu.VMEM((count, block), jnp.bfloat16),
                    pltpu.VMEM((count, teams * HEAD_SIZE), jnp.float32),
                ],
            ),
            out_shape=jax.ShapeDtypeStruct((teams, count, HEAD_SIZE), jnp.float32),
            cost_estimate=pl.CostEstimate(
                flops=2 * count * block * teams * HEAD_SIZE,
                bytes_accessed=2 * block * (count + teams * HEAD_SIZE),
                transcendentals=0,
            ),
        )(pos, passage_hidden_states, *others, *tails, *weights)

    def summed(parts, kind):
        total = parts[0]
        for ka in range(1, teams):
            total = total + swap(parts[ka].astype(kind), ka * ring).astype(jnp.float32)
        return total

    key_rows = summed(project(keys_w, "key_parts"), WIRE)
    value_rows = summed(project(values_w, "value_parts"), jnp.bfloat16).astype(jnp.bfloat16)

    stored = jnp.arange(teams * rows, dtype=jnp.int32)
    row_ids = (stored // rows * ring + seat) * rows + stored % rows
    places = positions_of(row_ids, lengths, storage_order, orders).reshape(-1)
    tail_places = total_keys + seat * mine + jnp.arange(mine, dtype=jnp.int32)
    key_cos, key_sin = turn_tables(jnp.concatenate([places, tail_places]))
    query_places = total_keys + jnp.arange(heads * tokens, dtype=jnp.int32) % tokens
    query_cos, query_sin = turn_tables(query_places)

    packed = pl.pallas_call(
        functools.partial(pack_kernel, perms),
        name="pack_rows",
        in_specs=in_vmem(4),
        out_specs=pl.BlockSpec(memory_space=pltpu.VMEM),
        out_shape=jax.ShapeDtypeStruct(
            ((perms + 1) * teams * rows + 2 * mine, HEAD_SIZE), jnp.bfloat16
        ),
    )(key_rows, value_rows, key_cos, key_sin)
    pieces = gathered(packed)

    count = heads * tokens
    attended = pl.pallas_call(
        functools.partial(attend_kernel, perms, ring, teams * rows, tokens),
        name="attend",
        grid_spec=pltpu.PrefetchScalarGridSpec(
            num_scalar_prefetch=1,
            grid=(1,),
            in_specs=in_vmem(3 + ring),
            out_specs=pl.BlockSpec(memory_space=pltpu.VMEM),
            scratch_shapes=[
                pltpu.VMEM((tokens, HEAD_SIZE), jnp.bfloat16),
                pltpu.VMEM((tokens, HEAD_SIZE), jnp.bfloat16),
                pltpu.VMEM((count, total_keys), jnp.float32),
            ],
        ),
        out_shape=jax.ShapeDtypeStruct((count, HEAD_SIZE), jnp.bfloat16),
    )(pos, query, query_cos, query_sin, *pieces)

    column = jnp.stack([attended] + [swap(attended, ka * ring) for ka in range(1, teams)])
    projected, squares = pl.pallas_call(
        functools.partial(output_kernel, teams, ring, tokens),
        name="output_parts",
        grid_spec=pltpu.PrefetchScalarGridSpec(
            num_scalar_prefetch=1,
            grid=(1,),
            in_specs=in_vmem(ring + 1),
            out_specs=in_vmem(2),
        ),
        out_shape=[
            jax.ShapeDtypeStruct((tokens, w_out.shape[1]), jnp.float32),
            jax.ShapeDtypeStruct((8, tokens), jnp.float32),
        ],
    )(pos, *gathered(column), w_out)
    bit = 1
    while bit < shards:
        squares = squares + swap(squares, bit)
        bit *= 2
    factor = lax.rsqrt(squares[0] / MODEL_WIDTH + epsilon)[:, None]
    return (projected * factor * norm_gain[None, :]).astype(jnp.bfloat16)


def power_of_two(number):
    return number & (number - 1) == 0


def per_device(*args):
    tail, weight = args[0], args[6]
    shards = lax.axis_size("psg")
    teams = weight.shape[1] // HEAD_SIZE
    ring = shards // teams
    if (
        shards % teams == 0
        and power_of_two(shards)
        and power_of_two(teams)
        and ring > 1
        and args[5].shape[1] % (HEAD_SIZE * shards) == 0
        and tail.shape[1] % HEAD_SIZE == 0
        and tail.shape[0] % (16 * ring) == 0
        and power_of_two(tail.shape[0])
        and args[1].shape[0] % 16 == 0
    ):
        return split_device(*args)
    return general_device(*args)


def solution(mesh):
    placed = (
        P("groups", "psg"),
        P(("groups", "psg"), None),
        P("groups"),
        P("groups"),
        P("groups", None),
        P("psg", None),
        P("psg", None),
        P("psg", None),
        P(None, "psg"),
        P("psg"),
    )
    return jax.shard_map(
        per_device, mesh=mesh, in_specs=placed, out_specs=P("groups", "psg"), check_vma=False
    )
```

```python
import functools

import jax
import jax.numpy as jnp
import numpy as np
from jax import lax
from jax.experimental import pallas as pl
from jax.experimental.pallas import tpu as pltpu
from jax.sharding import PartitionSpec as P


MODEL_WIDTH = 8192
HEAD_SIZE = 128


theta_base = 500000.0
epsilon = 1e-05


def joined(part, axis, combine):
    gathered = jax.tree.map(lambda a: lax.all_gather(a, axis), part)

    def take(source):
        return jax.tree.map(lambda a: lax.dynamic_index_in_dim(a, source, 0, False), gathered)

    return lax.fori_loop(
        1, lax.axis_size(axis), lambda source, state: combine(state, take(source)), take(0)
    )


def rotate(vectors, places):
    half = vectors.shape[-1] // 2
    freqs = theta_base ** (-jnp.arange(half, dtype=jnp.float32) * 2.0 / vectors.shape[-1])
    angles = places.astype(jnp.float32)[:, None] * freqs[None, :]
    cosine = jnp.cos(angles)[:, None, :]
    sine = jnp.sin(angles)[:, None, :]
    first = vectors[..., :half]
    second = vectors[..., half:]
    return jnp.concatenate(
        [first * cosine - second * sine, second * cosine + first * sine], axis=-1
    )


def general_device(
    tail_hidden_states,
    passage_hidden_states,
    lengths,
    storage_order,
    orders,
    w_query,
    key_weight,
    value_weight,
    w_out,
    norm_gain,
):
    shards = lax.axis_size("psg")
    device = lax.axis_index("psg")
    row_count = passage_hidden_states.shape[0]
    tail_count = tail_hidden_states.shape[0]
    kv_heads = key_weight.shape[1] // HEAD_SIZE
    query_heads = w_query.shape[1] // HEAD_SIZE
    query_group = query_heads // kv_heads
    total_keys = row_count * shards
    query_part = jnp.dot(tail_hidden_states, w_query, preferred_element_type=jnp.float32)
    key_part = jnp.dot(tail_hidden_states, key_weight, preferred_element_type=jnp.float32)
    value_part = jnp.dot(tail_hidden_states, value_weight, preferred_element_type=jnp.float32)
    query_sum, key_sum, value_sum = lax.psum((query_part, key_part, value_part), "psg")
    tail_pos = total_keys + jnp.arange(tail_count, dtype=jnp.int32)
    query_vectors = rotate(query_sum.reshape(tail_count, query_heads, HEAD_SIZE), tail_pos).astype(
        jnp.bfloat16
    )
    query_vectors = query_vectors.reshape(tail_count, kv_heads, query_group, HEAD_SIZE)
    tail_key_rows = rotate(key_sum.reshape(tail_count, kv_heads, HEAD_SIZE), tail_pos).astype(
        jnp.bfloat16
    )
    tail_value_rows = value_sum.astype(jnp.bfloat16).reshape(tail_count, kv_heads, HEAD_SIZE)

    def add_block(piece):
        return jnp.dot(passage_hidden_states, piece, preferred_element_type=jnp.float32)

    unrotated_key = add_block(lax.all_gather(key_weight, "psg", axis=0, tiled=True))
    raw_value = add_block(lax.all_gather(value_weight, "psg", axis=0, tiled=True))
    numbers = jnp.arange(lengths.shape[0], dtype=jnp.int32)
    pick = (storage_order[:, None] == numbers[None, :]).astype(jnp.int32)
    stored_lengths = jnp.sum(pick * lengths[None, :], axis=1)
    ends = jnp.cumsum(stored_lengths)
    starts = ends - stored_lengths
    row_ids = device * row_count + jnp.arange(row_count, dtype=jnp.int32)
    slots = jnp.sum((ends[None, :] <= row_ids[:, None]).astype(jnp.int32), axis=1)
    in_slot = (slots[:, None] == numbers[None, :]).astype(jnp.int32)
    offsets = row_ids - jnp.sum(in_slot * starts[None, :], axis=1)
    passage_hot = jnp.dot(in_slot, pick)
    ordered_hot = (orders[:, :, None] == numbers[None, None, :]).astype(jnp.int32)
    ordered_lengths = jnp.sum(ordered_hot * lengths[None, None, :], axis=2)
    order_starts = jnp.cumsum(ordered_lengths, axis=1) - ordered_lengths
    placed = jnp.sum(ordered_hot * order_starts[:, :, None], axis=1)
    token_positions = (
        jnp.sum(passage_hot[None, :, :] * placed[:, None, :], axis=2) + offsets[None, :]
    )
    passage_values = raw_value.astype(jnp.bfloat16).reshape(row_count, kv_heads, HEAD_SIZE)
    unrotated_key = unrotated_key.reshape(row_count, kv_heads, HEAD_SIZE)
    scale = HEAD_SIZE ** (-0.5)
    tail_scores = (
        jnp.einsum(
            "tkgd,skd->tkgs", query_vectors, tail_key_rows, preferred_element_type=jnp.float32
        )
        * scale
    )
    causal = jnp.arange(tail_count)[None, :] <= jnp.arange(tail_count)[:, None]
    tail_scores = jnp.where(causal[:, None, None, :], tail_scores, -1e30)
    tail_top = jnp.max(tail_scores, axis=-1)

    def scores_for(places):
        keys = rotate(unrotated_key, places).astype(jnp.bfloat16)
        return (
            jnp.einsum("tkgd,nkd->tkgn", query_vectors, keys, preferred_element_type=jnp.float32)
            * scale
        )

    def local_stats(places):
        scores = scores_for(places)
        peak = jnp.maximum(jnp.max(scores, axis=-1), tail_top)
        return (peak, jnp.sum(jnp.exp(scores - peak[..., None]), axis=-1))

    def combine(first, second):
        peak = jnp.maximum(first[0], second[0])
        return (peak, first[1] * jnp.exp(first[0] - peak) + second[1] * jnp.exp(second[0] - peak))

    peaks, totals = joined(lax.map(local_stats, token_positions), "psg", combine)

    def accumulate(running, inputs):
        places, peak, partial_value = inputs
        weights = jnp.exp(scores_for(places) - peak[..., None])
        tail_weights = jnp.exp(tail_scores - peak[..., None])
        denom = (partial_value + jnp.sum(tail_weights, axis=-1))[..., None]
        shared = jnp.einsum(
            "tkgn,nkd->tkgd",
            weights.astype(jnp.bfloat16),
            passage_values,
            preferred_element_type=jnp.float32,
        )
        own = jnp.einsum(
            "tkgs,skd->tkgd",
            tail_weights.astype(jnp.bfloat16),
            tail_value_rows,
            preferred_element_type=jnp.float32,
        )
        return ((running[0] + shared / denom, running[1] + own / denom), None)

    start_sums = jnp.zeros((tail_count, kv_heads, query_group, HEAD_SIZE), jnp.float32)
    (shared_sum, own_sum), unused_slot = lax.scan(
        accumulate, (start_sums, start_sums), (token_positions, peaks, totals)
    )
    agreed_output = lax.psum(shared_sum, "psg") + own_sum
    mixed = agreed_output.reshape(tail_count, -1).astype(jnp.bfloat16)
    projected = jnp.dot(mixed, w_out, preferred_element_type=jnp.float32)
    squares = lax.psum(jnp.sum(projected * projected, axis=1), "psg")
    factor = lax.rsqrt(squares / MODEL_WIDTH + epsilon)[:, None]
    return (projected * factor * norm_gain[None, :]).astype(jnp.bfloat16)


WIRE = jnp.float16
ROWS_COLUMNS = (((1,), (1,)), ((), ()))


def granted(mebibytes):
    return pltpu.CompilerParams(vmem_limit_bytes=mebibytes << 20)


def in_vmem(count):
    return [pl.BlockSpec(memory_space=pltpu.VMEM)] * count


def table_kernel(teams, ring, rows, perms, pos, lengths, storage_order, orders, freq_ref, *out_refs):
    key_cos, key_sin, query_cos, query_sin = out_refs
    passages = lengths.shape[0]
    mine = key_cos.shape[0] - perms * teams * rows
    tokens = mine * ring
    stored = [storage_order[s] for s in range(passages)]
    starts = [jnp.int32(0)]
    for s in range(passages - 1):
        starts.append(starts[-1] + lengths[stored[s]])
    shifts = []
    for r in range(perms):
        first, placed = jnp.int32(0), [jnp.int32(0)] * passages
        for i in range(passages):
            passage = orders[r * passages + i]
            placed = [old + jnp.where(stored[s] == passage, first, 0) for s, old in enumerate(placed)]
            first = first + lengths[passage]
        shifts.append([placed[s] - starts[s] for s in range(passages)])
    lane = lax.broadcasted_iota(jnp.int32, (1, HEAD_SIZE), 1)
    sign = jnp.where(lane < HEAD_SIZE // 2, -1.0, 1.0)

    def write(cos_ref, sin_ref, first, places):
        angles = places.astype(jnp.float32) * freq_ref[...]
        place = slice(first, first + places.shape[0])
        cos_ref[place, :] = jnp.cos(angles)
        sin_ref[place, :] = jnp.sin(angles) * sign

    for ka in range(teams):
        ids = lax.broadcasted_iota(jnp.int32, (rows, HEAD_SIZE), 0) + (ka * ring + pos[1]) * rows
        for r in range(perms):
            shift = shifts[r][0]
            for s in range(1, passages):
                shift = jnp.where(ids >= starts[s], shifts[r][s], shift)
            write(key_cos, key_sin, (r * teams + ka) * rows, ids + shift)
    total = teams * ring * rows
    ids = lax.broadcasted_iota(jnp.int32, (mine, HEAD_SIZE), 0) + (total + pos[1] * mine)
    write(key_cos, key_sin, perms * teams * rows, ids)
    ids = lax.broadcasted_iota(jnp.int32, (tokens, HEAD_SIZE), 0) + total
    write(query_cos, query_sin, 0, ids)


def turned(vectors, cosine, sine):
    return vectors * cosine + pltpu.roll(vectors, HEAD_SIZE // 2, 1) * sine


def bit_order(count):
    width = count.bit_length() - 1
    return [int(format(s, "b").zfill(width)[::-1], 2) if width else 0 for s in range(count)]


def query_kernel(ring, heads, pos, x_ref, w_ref, keep_ref, send_ref, acc_ref):
    acc_ref[...] = jnp.dot(x_ref[...], w_ref[...], preferred_element_type=jnp.float32)
    tokens = x_ref.shape[0]
    for slot, kb in enumerate(bit_order(ring)):
        unit = pos[1] ^ kb
        out = keep_ref if slot < ring // 2 else send_ref
        for j in range(heads):
            column = pl.multiple_of((unit * heads + j) * HEAD_SIZE, HEAD_SIZE)
            out[slot % (ring // 2), 0, j * tokens : (j + 1) * tokens, :] = acc_ref[
                :, pl.ds(column, HEAD_SIZE)
            ]


def project(teams, ring, pos, rows_ref, w_refs, out_refs, acc_ref):
    width = w_refs[0].shape[0]
    total = None
    for kb in range(ring):
        part = jnp.dot(
            rows_ref[:, kb * width : (kb + 1) * width],
            w_refs[kb][...],
            preferred_element_type=jnp.float32,
        )
        total = part if total is None else total + part
    acc_ref[...] = total
    for ka in range(teams):
        column = pl.multiple_of((pos[0] ^ ka) * HEAD_SIZE, HEAD_SIZE)
        out_refs[ka][...] = acc_ref[:, pl.ds(column, HEAD_SIZE)].astype(out_refs[ka].dtype)


def key_kernel(teams, ring, pos, *refs):
    x_refs, t_refs, w_refs = refs[:teams], refs[teams : teams + ring], refs[teams + ring : teams + 2 * ring]
    *out_refs, all_ref, acc_ref = refs[teams + 2 * ring :]
    rows, width, mine = x_refs[0].shape[0], t_refs[0].shape[1], t_refs[0].shape[0] // ring
    for kb in range(ring):
        column = pl.multiple_of((pos[1] ^ kb) * width, width)
        place = slice(kb * width, (kb + 1) * width)
        for ka in range(teams):
            first = pl.multiple_of((pos[0] ^ ka) * rows, rows)
            all_ref[pl.ds(first, rows), place] = x_refs[ka][:, pl.ds(column, width)]
        first = pl.multiple_of(pos[1] * mine, mine)
        all_ref[teams * rows :, place] = t_refs[kb][pl.ds(first, mine), :]
    project(teams, ring, pos, all_ref, w_refs, out_refs, acc_ref)


def value_kernel(teams, ring, pos, rows_ref, *refs):
    project(teams, ring, pos, rows_ref, refs[:ring], refs[ring:-1], refs[-1])


def turn_kernel(perms, k_ref, cos_ref, sin_ref, out_ref):
    rows = (out_ref.shape[0] - k_ref.shape[0]) // (perms - 1)
    for r in range(perms):
        place = slice(r * rows, (r + 1) * rows)
        out_ref[place, :] = turned(k_ref[:rows, :], cos_ref[place, :], sin_ref[place, :]).astype(
            out_ref.dtype
        )
    out_ref[perms * rows :, :] = turned(
        k_ref[rows:, :], cos_ref[perms * rows :, :], sin_ref[perms * rows :, :]
    ).astype(out_ref.dtype)


def attend_kernel(perms, ring, rows, tokens, pos, q_ref, cos_ref, sin_ref, *refs):
    k_refs, v_refs = refs[:ring], refs[ring : 2 * ring]
    out_ref, tk_ref, tv_ref, score_ref = refs[2 * ring :]
    mine = tokens // ring
    base = perms * rows
    scale = HEAD_SIZE ** (-0.5)
    query = jnp.concatenate(
        [
            turned(q_ref[first : first + tokens, :], cos_ref[...], sin_ref[...])
            for first in range(0, q_ref.shape[0], tokens)
        ],
        axis=0,
    ).astype(jnp.bfloat16)
    for kb in range(ring):
        first = pl.multiple_of((pos[1] ^ kb) * mine, mine)
        tk_ref[pl.ds(first, mine), :] = k_refs[kb][base:, :]
        tv_ref[pl.ds(first, mine), :] = v_refs[kb][rows:, :]
    count = q_ref.shape[0]
    tail = (
        lax.dot_general(query, tk_ref[...], ROWS_COLUMNS, preferred_element_type=jnp.float32) * scale
    )
    token = lax.broadcasted_iota(jnp.int32, (count, tokens), 0) & (tokens - 1)
    tail = jnp.where(lax.broadcasted_iota(jnp.int32, (count, tokens), 1) <= token, tail, -1e30)
    tail_top = jnp.max(tail, axis=1, keepdims=True)
    agreed = None
    for r in range(perms):
        top = tail_top
        for kb in range(ring):
            part = (
                lax.dot_general(
                    query,
                    k_refs[kb][r * rows : (r + 1) * rows, :],
                    ROWS_COLUMNS,
                    preferred_element_type=jnp.float32,
                )
                * scale
            )
            score_ref[:, kb * rows : (kb + 1) * rows] = part
            top = jnp.maximum(top, jnp.max(part, axis=1, keepdims=True))
        weights = jnp.exp(tail - top)
        denom = jnp.sum(weights, axis=1, keepdims=True)
        mixed = jnp.dot(
            weights.astype(jnp.bfloat16), tv_ref[...], preferred_element_type=jnp.float32
        )
        for kb in range(ring):
            weights = jnp.exp(score_ref[:, kb * rows : (kb + 1) * rows] - top)
            denom = denom + jnp.sum(weights, axis=1, keepdims=True)
            mixed = mixed + jnp.dot(
                weights.astype(jnp.bfloat16),
                v_refs[kb][:rows, :],
                preferred_element_type=jnp.float32,
            )
        mixed = mixed / denom
        agreed = mixed if agreed is None else agreed + mixed
    out_ref[...] = agreed.astype(out_ref.dtype)


def output_kernel(teams, ring, tokens, pos, *refs):
    y_refs, (w_ref, out_ref, square_ref) = refs[:ring], refs[ring:]
    heads = y_refs[0].shape[1] // tokens
    total = None
    for kb in range(ring):
        for ka in range(teams):
            unit = (pos[0] ^ ka) * ring + (pos[1] ^ kb)
            first = pl.multiple_of(unit * heads * HEAD_SIZE, HEAD_SIZE)
            left = jnp.concatenate(
                [y_refs[kb][ka, j * tokens : (j + 1) * tokens, :] for j in range(heads)], axis=1
            )
            part = jnp.dot(
                left, w_ref[pl.ds(first, heads * HEAD_SIZE), :], preferred_element_type=jnp.float32
            )
            total = part if total is None else total + part
    out_ref[...] = total
    square_ref[...] = lax.dot_general(
        jnp.ones((8, total.shape[1]), jnp.float32),
        total * total,
        ROWS_COLUMNS,
        precision=lax.Precision.HIGHEST,
        preferred_element_type=jnp.float32,
    )


def split_device(
    tail_hidden_states,
    passage_hidden_states,
    lengths,
    storage_order,
    orders,
    w_query,
    key_weight,
    value_weight,
    w_out,
    norm_gain,
):
    shards = lax.axis_size("psg")
    device = lax.axis_index("psg")
    teams = key_weight.shape[1] // HEAD_SIZE
    ring = shards // teams
    tokens, width = tail_hidden_states.shape
    rows = passage_hidden_states.shape[0]
    mine = tokens // ring
    team, seat = device // ring, device % ring
    perms = orders.shape[0]
    heads = w_query.shape[1] // (HEAD_SIZE * shards)
    total_keys = rows * shards
    block = width * ring
    pos = jnp.stack([team, seat]).astype(jnp.int32)

    def swap(x, k):
        return lax.ppermute(x, "psg", [(i, i ^ k) for i in range(shards)])

    def gathered(x):
        pieces, bit = {0: x}, ring // 2
        while bit:
            for kb, piece in list(pieces.items()):
                pieces[kb | bit] = swap(piece, bit)
            bit //= 2
        return [pieces[kb] for kb in range(ring)]

    def exchanged(parts):
        return [swap(part, (ka + 1) * ring) for ka, part in enumerate(parts)]

    def chunk(ka):
        return lax.dynamic_slice_in_dim(passage_hidden_states, (team ^ ka) * block, block, 1)

    others = exchanged([chunk(ka) for ka in range(1, teams)])
    keys_w = gathered(key_weight)
    tails = gathered(tail_hidden_states)
    values_w = gathered(value_weight)

    units = w_query.shape[1] // teams
    part_shape = jax.ShapeDtypeStruct((ring // 2, teams, heads * tokens, HEAD_SIZE), jnp.float32)
    part_spec = pl.BlockSpec((ring // 2, 1, heads * tokens, HEAD_SIZE), lambda i, pos: (0, i, 0, 0))
    keep, send = pl.pallas_call(
        functools.partial(query_kernel, ring, heads),
        name="query_parts",
        compiler_params=granted(10),
        grid_spec=pltpu.PrefetchScalarGridSpec(
            num_scalar_prefetch=1,
            grid=(teams,),
            in_specs=[
                pl.BlockSpec((tokens, width), lambda i, pos: (0, 0)),
                pl.BlockSpec((width, units), lambda i, pos: (0, pos[0] ^ i)),
            ],
            out_specs=[part_spec, part_spec],
            scratch_shapes=[pltpu.VMEM((tokens, units), jnp.float32)],
        ),
        out_shape=[part_shape, part_shape],
        cost_estimate=pl.CostEstimate(
            flops=2 * tokens * width * units * teams,
            bytes_accessed=2 * width * units * teams,
            transcendentals=0,
        ),
    )(pos, tail_hidden_states, w_query)
    bit = 1
    while True:
        query_part = keep + swap(send, bit).astype(jnp.float32)
        bit *= 2
        if bit == ring:
            break
        half = query_part.shape[0] // 2
        keep, send = query_part[:half], query_part[half:].astype(WIRE)
    query_part = query_part[0]

    half = HEAD_SIZE // 2
    freqs = (theta_base ** (-np.arange(half) * 2.0 / HEAD_SIZE)).astype(np.float32)
    key_table = jax.ShapeDtypeStruct((perms * teams * rows + mine, HEAD_SIZE), jnp.float32)
    query_table = jax.ShapeDtypeStruct((tokens, HEAD_SIZE), jnp.float32)
    key_cos, key_sin, query_cos, query_sin = pl.pallas_call(
        functools.partial(table_kernel, teams, ring, rows, perms),
        name="tables",
        compiler_params=granted(6),
        grid_spec=pltpu.PrefetchScalarGridSpec(
            num_scalar_prefetch=4,
            grid=(1,),
            in_specs=in_vmem(1),
            out_specs=in_vmem(4),
        ),
        out_shape=[key_table, key_table, query_table, query_table],
        cost_estimate=pl.CostEstimate(
            flops=key_table.size * 100, bytes_accessed=key_table.size * 8, transcendentals=0
        ),
    )(pos, lengths, storage_order, orders.reshape(-1), jnp.asarray(np.tile(freqs, 2)[None, :]))

    count = teams * rows + mine
    cost = pl.CostEstimate(
        flops=2 * count * block * teams * HEAD_SIZE,
        bytes_accessed=2 * block * (count + teams * HEAD_SIZE),
        transcendentals=0,
    )
    own_shape = jax.ShapeDtypeStruct((count, HEAD_SIZE), jnp.float32)
    acc_shape = pltpu.VMEM((count, teams * HEAD_SIZE), jnp.float32)
    *key_parts, all_rows = pl.pallas_call(
        functools.partial(key_kernel, teams, ring),
        name="key_parts",
        compiler_params=granted(14),
        grid_spec=pltpu.PrefetchScalarGridSpec(
            num_scalar_prefetch=1,
            grid=(1,),
            in_specs=in_vmem(teams + 2 * ring),
            out_specs=in_vmem(teams + 1),
            scratch_shapes=[acc_shape],
        ),
        out_shape=[own_shape] * teams + [jax.ShapeDtypeStruct((count, block), jnp.bfloat16)],
        cost_estimate=cost,
    )(pos, chunk(0), *others, *tails, *keys_w)
    key_others = exchanged([part.astype(WIRE) for part in key_parts[1:]])
    value_parts = pl.pallas_call(
        functools.partial(value_kernel, teams, ring),
        name="value_parts",
        compiler_params=granted(10),
        grid_spec=pltpu.PrefetchScalarGridSpec(
            num_scalar_prefetch=1,
            grid=(1,),
            in_specs=in_vmem(1 + ring),
            out_specs=in_vmem(teams),
            scratch_shapes=[acc_shape],
        ),
        out_shape=[own_shape]
        + [jax.ShapeDtypeStruct(own_shape.shape, jnp.bfloat16)] * (teams - 1),
        cost_estimate=cost,
    )(pos, all_rows, *values_w)
    value_others = exchanged(value_parts[1:])

    def summed(own, others):
        for part in others:
            own = own + part.astype(jnp.float32)
        return own

    key_rows = summed(key_parts[0], key_others)
    turned_keys = pl.pallas_call(
        functools.partial(turn_kernel, perms),
        name="turn_keys",
        compiler_params=granted(6),
        in_specs=in_vmem(3),
        out_specs=pl.BlockSpec(memory_space=pltpu.VMEM),
        out_shape=jax.ShapeDtypeStruct((perms * teams * rows + mine, HEAD_SIZE), jnp.bfloat16),
    )(key_rows, key_cos, key_sin)
    key_pieces = gathered(turned_keys)
    value_rows = summed(value_parts[0], value_others).astype(jnp.bfloat16)
    value_pieces = gathered(value_rows)
    query_others = exchanged([part.astype(WIRE) for part in query_part[1:]])
    query = summed(query_part[0], query_others)

    count = heads * tokens
    attended = pl.pallas_call(
        functools.partial(attend_kernel, perms, ring, teams * rows, tokens),
        name="attend",
        compiler_params=granted(14),
        grid_spec=pltpu.PrefetchScalarGridSpec(
            num_scalar_prefetch=1,
            grid=(1,),
            in_specs=in_vmem(3 + 2 * ring),
            out_specs=pl.BlockSpec(memory_space=pltpu.VMEM),
            scratch_shapes=[
                pltpu.VMEM((tokens, HEAD_SIZE), jnp.bfloat16),
                pltpu.VMEM((tokens, HEAD_SIZE), jnp.bfloat16),
                pltpu.VMEM((count, total_keys), jnp.float32),
            ],
        ),
        out_shape=jax.ShapeDtypeStruct((count, HEAD_SIZE), jnp.bfloat16),
    )(pos, query, query_cos, query_sin, *key_pieces, *value_pieces)

    column = jnp.stack([attended] + exchanged([attended] * (teams - 1)))
    projected, squares = pl.pallas_call(
        functools.partial(output_kernel, teams, ring, tokens),
        name="output_parts",
        compiler_params=granted(12),
        grid_spec=pltpu.PrefetchScalarGridSpec(
            num_scalar_prefetch=1,
            grid=(1,),
            in_specs=in_vmem(ring + 1),
            out_specs=in_vmem(2),
        ),
        out_shape=[
            jax.ShapeDtypeStruct((tokens, w_out.shape[1]), jnp.float32),
            jax.ShapeDtypeStruct((8, tokens), jnp.float32),
        ],
    )(pos, *gathered(column), w_out)
    bit = 1
    while bit < shards:
        squares = squares + swap(squares, bit)
        bit *= 2
    factor = lax.rsqrt(squares[0] / MODEL_WIDTH + epsilon)[:, None]
    return (projected * factor * norm_gain[None, :]).astype(jnp.bfloat16)


def power_of_two(number):
    return number & (number - 1) == 0


def splits(shards, args):
    tail, weight = args[0], args[6]
    teams = weight.shape[1] // HEAD_SIZE
    ring = shards // teams
    return (
        shards % teams == 0
        and power_of_two(shards)
        and power_of_two(teams)
        and ring > 1
        and args[5].shape[1] % (HEAD_SIZE * shards) == 0
        and tail.shape[1] % HEAD_SIZE == 0
        and tail.shape[0] % (16 * ring) == 0
        and power_of_two(tail.shape[0])
        and args[1].shape[0] % 16 == 0
    )


def per_device(*args):
    if splits(lax.axis_size("psg"), args):
        return split_device(*args)
    return general_device(*args)


def solution(mesh):
    placed = (
        P("groups", "psg"),
        P(("groups", "psg"), None),
        P("groups"),
        P("groups"),
        P("groups", None),
        P("psg", None),
        P("psg", None),
        P("psg", None),
        P(None, "psg"),
        P("psg"),
    )
    return jax.shard_map(
        per_device, mesh=mesh, in_specs=placed, out_specs=P("groups", "psg"), check_vma=False
    )
```

```python
import functools

import jax
import jax.numpy as jnp
import numpy as np
from jax import lax
from jax.experimental import pallas as pl
from jax.experimental.pallas import tpu as pltpu
from jax.sharding import PartitionSpec as P


MODEL_WIDTH = 8192
HEAD_SIZE = 128


theta_base = 500000.0
epsilon = 1e-05


def joined(part, axis, combine):
    gathered = jax.tree.map(lambda a: lax.all_gather(a, axis), part)

    def take(source):
        return jax.tree.map(lambda a: lax.dynamic_index_in_dim(a, source, 0, False), gathered)

    return lax.fori_loop(
        1, lax.axis_size(axis), lambda source, state: combine(state, take(source)), take(0)
    )


def rotate(vectors, places):
    half = vectors.shape[-1] // 2
    freqs = theta_base ** (-jnp.arange(half, dtype=jnp.float32) * 2.0 / vectors.shape[-1])
    angles = places.astype(jnp.float32)[:, None] * freqs[None, :]
    cosine = jnp.cos(angles)[:, None, :]
    sine = jnp.sin(angles)[:, None, :]
    first = vectors[..., :half]
    second = vectors[..., half:]
    return jnp.concatenate(
        [first * cosine - second * sine, second * cosine + first * sine], axis=-1
    )


def general_device(
    tail_hidden_states,
    passage_hidden_states,
    lengths,
    storage_order,
    orders,
    w_query,
    key_weight,
    value_weight,
    w_out,
    norm_gain,
):
    shards = lax.axis_size("psg")
    device = lax.axis_index("psg")
    row_count = passage_hidden_states.shape[0]
    tail_count = tail_hidden_states.shape[0]
    kv_heads = key_weight.shape[1] // HEAD_SIZE
    query_heads = w_query.shape[1] // HEAD_SIZE
    query_group = query_heads // kv_heads
    total_keys = row_count * shards
    query_part = jnp.dot(tail_hidden_states, w_query, preferred_element_type=jnp.float32)
    key_part = jnp.dot(tail_hidden_states, key_weight, preferred_element_type=jnp.float32)
    value_part = jnp.dot(tail_hidden_states, value_weight, preferred_element_type=jnp.float32)
    query_sum, key_sum, value_sum = lax.psum((query_part, key_part, value_part), "psg")
    tail_pos = total_keys + jnp.arange(tail_count, dtype=jnp.int32)
    query_vectors = rotate(query_sum.reshape(tail_count, query_heads, HEAD_SIZE), tail_pos).astype(
        jnp.bfloat16
    )
    query_vectors = query_vectors.reshape(tail_count, kv_heads, query_group, HEAD_SIZE)
    tail_key_rows = rotate(key_sum.reshape(tail_count, kv_heads, HEAD_SIZE), tail_pos).astype(
        jnp.bfloat16
    )
    tail_value_rows = value_sum.astype(jnp.bfloat16).reshape(tail_count, kv_heads, HEAD_SIZE)

    def add_block(piece):
        return jnp.dot(passage_hidden_states, piece, preferred_element_type=jnp.float32)

    unrotated_key = add_block(lax.all_gather(key_weight, "psg", axis=0, tiled=True))
    raw_value = add_block(lax.all_gather(value_weight, "psg", axis=0, tiled=True))
    numbers = jnp.arange(lengths.shape[0], dtype=jnp.int32)
    pick = (storage_order[:, None] == numbers[None, :]).astype(jnp.int32)
    stored_lengths = jnp.sum(pick * lengths[None, :], axis=1)
    ends = jnp.cumsum(stored_lengths)
    starts = ends - stored_lengths
    row_ids = device * row_count + jnp.arange(row_count, dtype=jnp.int32)
    slots = jnp.sum((ends[None, :] <= row_ids[:, None]).astype(jnp.int32), axis=1)
    in_slot = (slots[:, None] == numbers[None, :]).astype(jnp.int32)
    offsets = row_ids - jnp.sum(in_slot * starts[None, :], axis=1)
    passage_hot = jnp.dot(in_slot, pick)
    ordered_hot = (orders[:, :, None] == numbers[None, None, :]).astype(jnp.int32)
    ordered_lengths = jnp.sum(ordered_hot * lengths[None, None, :], axis=2)
    order_starts = jnp.cumsum(ordered_lengths, axis=1) - ordered_lengths
    placed = jnp.sum(ordered_hot * order_starts[:, :, None], axis=1)
    token_positions = (
        jnp.sum(passage_hot[None, :, :] * placed[:, None, :], axis=2) + offsets[None, :]
    )
    passage_values = raw_value.astype(jnp.bfloat16).reshape(row_count, kv_heads, HEAD_SIZE)
    unrotated_key = unrotated_key.reshape(row_count, kv_heads, HEAD_SIZE)
    scale = HEAD_SIZE ** (-0.5)
    tail_scores = (
        jnp.einsum(
            "tkgd,skd->tkgs", query_vectors, tail_key_rows, preferred_element_type=jnp.float32
        )
        * scale
    )
    causal = jnp.arange(tail_count)[None, :] <= jnp.arange(tail_count)[:, None]
    tail_scores = jnp.where(causal[:, None, None, :], tail_scores, -1e30)
    tail_top = jnp.max(tail_scores, axis=-1)

    def scores_for(places):
        keys = rotate(unrotated_key, places).astype(jnp.bfloat16)
        return (
            jnp.einsum("tkgd,nkd->tkgn", query_vectors, keys, preferred_element_type=jnp.float32)
            * scale
        )

    def local_stats(places):
        scores = scores_for(places)
        peak = jnp.maximum(jnp.max(scores, axis=-1), tail_top)
        return (peak, jnp.sum(jnp.exp(scores - peak[..., None]), axis=-1))

    def combine(first, second):
        peak = jnp.maximum(first[0], second[0])
        return (peak, first[1] * jnp.exp(first[0] - peak) + second[1] * jnp.exp(second[0] - peak))

    peaks, totals = joined(lax.map(local_stats, token_positions), "psg", combine)

    def accumulate(running, inputs):
        places, peak, partial_value = inputs
        weights = jnp.exp(scores_for(places) - peak[..., None])
        tail_weights = jnp.exp(tail_scores - peak[..., None])
        denom = (partial_value + jnp.sum(tail_weights, axis=-1))[..., None]
        shared = jnp.einsum(
            "tkgn,nkd->tkgd",
            weights.astype(jnp.bfloat16),
            passage_values,
            preferred_element_type=jnp.float32,
        )
        own = jnp.einsum(
            "tkgs,skd->tkgd",
            tail_weights.astype(jnp.bfloat16),
            tail_value_rows,
            preferred_element_type=jnp.float32,
        )
        return ((running[0] + shared / denom, running[1] + own / denom), None)

    start_sums = jnp.zeros((tail_count, kv_heads, query_group, HEAD_SIZE), jnp.float32)
    (shared_sum, own_sum), unused_slot = lax.scan(
        accumulate, (start_sums, start_sums), (token_positions, peaks, totals)
    )
    agreed_output = lax.psum(shared_sum, "psg") + own_sum
    mixed = agreed_output.reshape(tail_count, -1).astype(jnp.bfloat16)
    projected = jnp.dot(mixed, w_out, preferred_element_type=jnp.float32)
    squares = lax.psum(jnp.sum(projected * projected, axis=1), "psg")
    factor = lax.rsqrt(squares / MODEL_WIDTH + epsilon)[:, None]
    return (projected * factor * norm_gain[None, :]).astype(jnp.bfloat16)


WIRE = jnp.float16
ROWS_COLUMNS = (((1,), (1,)), ((), ()))


def granted(mebibytes):
    return pltpu.CompilerParams(vmem_limit_bytes=mebibytes << 20)


def team_at(team, steps, teams):
    return (team + steps) & (teams - 1)


def in_vmem(count):
    return [pl.BlockSpec(memory_space=pltpu.VMEM)] * count


def table_kernel(teams, ring, rows, perms, pos, lengths, storage_order, orders, freq_ref, *out_refs):
    key_cos, key_sin, query_cos, query_sin = out_refs
    passages = lengths.shape[0]
    mine = key_cos.shape[0] - perms * teams * rows
    tokens = mine * ring
    stored = [storage_order[s] for s in range(passages)]
    starts = [jnp.int32(0)]
    for s in range(passages - 1):
        starts.append(starts[-1] + lengths[stored[s]])
    shifts = []
    for r in range(perms):
        first, placed = jnp.int32(0), [jnp.int32(0)] * passages
        for i in range(passages):
            passage = orders[r * passages + i]
            placed = [old + jnp.where(stored[s] == passage, first, 0) for s, old in enumerate(placed)]
            first = first + lengths[passage]
        shifts.append([placed[s] - starts[s] for s in range(passages)])
    lane = lax.broadcasted_iota(jnp.int32, (1, HEAD_SIZE), 1)
    sign = jnp.where(lane < HEAD_SIZE // 2, -1.0, 1.0)

    def write(cos_ref, sin_ref, first, places):
        angles = places.astype(jnp.float32) * freq_ref[...]
        place = slice(first, first + places.shape[0])
        cos_ref[place, :] = jnp.cos(angles)
        sin_ref[place, :] = jnp.sin(angles) * sign

    for ka in range(teams):
        ids = lax.broadcasted_iota(jnp.int32, (rows, HEAD_SIZE), 0) + (ka * ring + pos[1]) * rows
        for r in range(perms):
            shift = shifts[r][0]
            for s in range(1, passages):
                shift = jnp.where(ids >= starts[s], shifts[r][s], shift)
            write(key_cos, key_sin, (r * teams + ka) * rows, ids + shift)
    total = teams * ring * rows
    ids = lax.broadcasted_iota(jnp.int32, (mine, HEAD_SIZE), 0) + (total + pos[1] * mine)
    write(key_cos, key_sin, perms * teams * rows, ids)
    ids = lax.broadcasted_iota(jnp.int32, (tokens, HEAD_SIZE), 0) + total
    write(query_cos, query_sin, 0, ids)


def turned(vectors, cosine, sine):
    return vectors * cosine + pltpu.roll(vectors, HEAD_SIZE // 2, 1) * sine


def bit_order(count):
    width = count.bit_length() - 1
    return [int(format(s, "b").zfill(width)[::-1], 2) if width else 0 for s in range(count)]


def query_kernel(ring, heads, pos, x_ref, w_ref, keep_ref, send_ref, acc_ref):
    acc_ref[...] = jnp.dot(x_ref[...], w_ref[...], preferred_element_type=jnp.float32)
    tokens = x_ref.shape[0]
    for slot, kb in enumerate(bit_order(ring)):
        unit = pos[1] ^ kb
        out = keep_ref if slot < ring // 2 else send_ref
        for j in range(heads):
            column = pl.multiple_of((unit * heads + j) * HEAD_SIZE, HEAD_SIZE)
            out[slot % (ring // 2), 0, j * tokens : (j + 1) * tokens, :] = acc_ref[
                :, pl.ds(column, HEAD_SIZE)
            ]


def project(teams, ring, pos, rows_ref, w_refs, out_refs, acc_ref):
    width = w_refs[0].shape[0]
    total = None
    for kb in range(ring):
        part = jnp.dot(
            rows_ref[:, kb * width : (kb + 1) * width],
            w_refs[kb][...],
            preferred_element_type=jnp.float32,
        )
        total = part if total is None else total + part
    acc_ref[...] = total
    for ka in range(teams):
        column = pl.multiple_of(team_at(pos[0], ka, teams) * HEAD_SIZE, HEAD_SIZE)
        out_refs[ka][...] = acc_ref[:, pl.ds(column, HEAD_SIZE)].astype(out_refs[ka].dtype)


def key_kernel(teams, ring, pos, *refs):
    x_refs, t_refs, w_refs = refs[:teams], refs[teams : teams + ring], refs[teams + ring : teams + 2 * ring]
    *out_refs, all_ref, acc_ref = refs[teams + 2 * ring :]
    rows, width, mine = x_refs[0].shape[0], t_refs[0].shape[1], t_refs[0].shape[0] // ring
    for kb in range(ring):
        column = pl.multiple_of((pos[1] ^ kb) * width, width)
        place = slice(kb * width, (kb + 1) * width)
        for ka in range(teams):
            first = pl.multiple_of(team_at(pos[0], -ka, teams) * rows, rows)
            all_ref[pl.ds(first, rows), place] = x_refs[ka][:, pl.ds(column, width)]
        first = pl.multiple_of(pos[1] * mine, mine)
        all_ref[teams * rows :, place] = t_refs[kb][pl.ds(first, mine), :]
    project(teams, ring, pos, all_ref, w_refs, out_refs, acc_ref)


def value_kernel(teams, ring, pos, rows_ref, *refs):
    project(teams, ring, pos, rows_ref, refs[:ring], refs[ring:-1], refs[-1])


def turn_kernel(perms, k_ref, cos_ref, sin_ref, out_ref):
    rows = (out_ref.shape[0] - k_ref.shape[0]) // (perms - 1)
    for r in range(perms):
        place = slice(r * rows, (r + 1) * rows)
        out_ref[place, :] = turned(k_ref[:rows, :], cos_ref[place, :], sin_ref[place, :]).astype(
            out_ref.dtype
        )
    out_ref[perms * rows :, :] = turned(
        k_ref[rows:, :], cos_ref[perms * rows :, :], sin_ref[perms * rows :, :]
    ).astype(out_ref.dtype)


def attend_kernel(perms, ring, rows, tokens, pos, q_ref, cos_ref, sin_ref, *refs):
    k_refs, v_refs = refs[:ring], refs[ring : 2 * ring]
    out_ref, tk_ref, tv_ref, score_ref = refs[2 * ring :]
    mine = tokens // ring
    base = perms * rows
    scale = HEAD_SIZE ** (-0.5)
    query = jnp.concatenate(
        [
            turned(q_ref[first : first + tokens, :], cos_ref[...], sin_ref[...])
            for first in range(0, q_ref.shape[0], tokens)
        ],
        axis=0,
    ).astype(jnp.bfloat16)
    for kb in range(ring):
        first = pl.multiple_of((pos[1] ^ kb) * mine, mine)
        tk_ref[pl.ds(first, mine), :] = k_refs[kb][base:, :]
        tv_ref[pl.ds(first, mine), :] = v_refs[kb][rows:, :]
    count = q_ref.shape[0]
    tail = (
        lax.dot_general(query, tk_ref[...], ROWS_COLUMNS, preferred_element_type=jnp.float32) * scale
    )
    token = lax.broadcasted_iota(jnp.int32, (count, tokens), 0) & (tokens - 1)
    tail = jnp.where(lax.broadcasted_iota(jnp.int32, (count, tokens), 1) <= token, tail, -1e30)
    tail_top = jnp.max(tail, axis=1, keepdims=True)
    agreed = None
    for r in range(perms):
        top = tail_top
        for kb in range(ring):
            part = (
                lax.dot_general(
                    query,
                    k_refs[kb][r * rows : (r + 1) * rows, :],
                    ROWS_COLUMNS,
                    preferred_element_type=jnp.float32,
                )
                * scale
            )
            score_ref[:, kb * rows : (kb + 1) * rows] = part
            top = jnp.maximum(top, jnp.max(part, axis=1, keepdims=True))
        weights = jnp.exp(tail - top)
        denom = jnp.sum(weights, axis=1, keepdims=True)
        mixed = jnp.dot(
            weights.astype(jnp.bfloat16), tv_ref[...], preferred_element_type=jnp.float32
        )
        for kb in range(ring):
            weights = jnp.exp(score_ref[:, kb * rows : (kb + 1) * rows] - top)
            denom = denom + jnp.sum(weights, axis=1, keepdims=True)
            mixed = mixed + jnp.dot(
                weights.astype(jnp.bfloat16),
                v_refs[kb][:rows, :],
                preferred_element_type=jnp.float32,
            )
        mixed = mixed / denom
        agreed = mixed if agreed is None else agreed + mixed
    out_ref[...] = agreed.astype(out_ref.dtype)


def output_kernel(units, teams, ring, tokens, first_part, pos, *refs):
    y_refs, w_ref, refs = refs[: len(units)], refs[len(units)], refs[len(units) + 1 :]
    heads = y_refs[0].shape[0] // tokens
    total = None if first_part else refs[0][...]
    for (kb, ka), y_ref in zip(units, y_refs, strict=True):
        unit = team_at(pos[0], -ka, teams) * ring + (pos[1] ^ kb)
        first = pl.multiple_of(unit * heads * HEAD_SIZE, HEAD_SIZE)
        left = jnp.concatenate(
            [y_ref[j * tokens : (j + 1) * tokens, :] for j in range(heads)], axis=1
        )
        part = jnp.dot(
            left, w_ref[pl.ds(first, heads * HEAD_SIZE), :], preferred_element_type=jnp.float32
        )
        total = part if total is None else total + part
    if first_part:
        refs[0][...] = total
        return
    refs[1][...] = total
    refs[2][...] = lax.dot_general(
        jnp.ones((8, total.shape[1]), jnp.float32),
        total * total,
        ROWS_COLUMNS,
        precision=lax.Precision.HIGHEST,
        preferred_element_type=jnp.float32,
    )


def split_device(
    tail_hidden_states,
    passage_hidden_states,
    lengths,
    storage_order,
    orders,
    w_query,
    key_weight,
    value_weight,
    w_out,
    norm_gain,
):
    shards = lax.axis_size("psg")
    device = lax.axis_index("psg")
    teams = key_weight.shape[1] // HEAD_SIZE
    ring = shards // teams
    tokens, width = tail_hidden_states.shape
    rows = passage_hidden_states.shape[0]
    mine = tokens // ring
    team, seat = device // ring, device % ring
    perms = orders.shape[0]
    heads = w_query.shape[1] // (HEAD_SIZE * shards)
    total_keys = rows * shards
    block = width * ring
    pos = jnp.stack([team, seat]).astype(jnp.int32)

    def swap(x, k):
        return lax.ppermute(x, "psg", [(i, i ^ k) for i in range(shards)])

    def gathered(x):
        pieces, bit = {0: x}, ring // 2
        while bit:
            for kb, piece in list(pieces.items()):
                pieces[kb | bit] = swap(piece, bit)
            bit //= 2
        return [pieces[kb] for kb in range(ring)]

    def exchanged(parts):
        moved = []
        for ka, part in enumerate(parts, 1):
            pairs = [(i, (i + ka * ring) % shards) for i in range(shards)]
            moved.append(lax.ppermute(part, "psg", pairs))
        return moved

    chunks = [
        lax.dynamic_slice_in_dim(
            passage_hidden_states, team_at(team, ka, teams) * block, block, 1
        )
        for ka in range(teams)
    ]
    others = exchanged(chunks[1:])
    keys_w = gathered(key_weight)
    tails = gathered(tail_hidden_states)
    values_w = gathered(value_weight)

    units = w_query.shape[1] // teams
    part_shape = jax.ShapeDtypeStruct((ring // 2, teams, heads * tokens, HEAD_SIZE), jnp.float32)
    part_spec = pl.BlockSpec((ring // 2, 1, heads * tokens, HEAD_SIZE), lambda i, pos: (0, i, 0, 0))
    keep, send = pl.pallas_call(
        functools.partial(query_kernel, ring, heads),
        name="qp",
        compiler_params=granted(10),
        grid_spec=pltpu.PrefetchScalarGridSpec(
            num_scalar_prefetch=1,
            grid=(teams,),
            in_specs=[
                pl.BlockSpec((tokens, width), lambda i, pos: (0, 0)),
                pl.BlockSpec((width, units), lambda i, pos: (0, team_at(pos[0], i, teams))),
            ],
            out_specs=[part_spec, part_spec],
            scratch_shapes=[pltpu.VMEM((tokens, units), jnp.float32)],
        ),
        out_shape=[part_shape, part_shape],
        cost_estimate=pl.CostEstimate(
            flops=2 * tokens * width * units * teams,
            bytes_accessed=2 * width * units * teams,
            transcendentals=0,
        ),
    )(pos, tail_hidden_states, pltpu.with_memory_space_constraint(w_query, pltpu.HBM))
    bit = 1
    while True:
        arrived = swap(send, bit)
        query_part = keep + arrived.astype(jnp.float32)
        bit *= 2
        if bit == ring:
            break
        half = query_part.shape[0] // 2
        keep, send = query_part[:half], query_part[half:].astype(WIRE)
    query_part = query_part[0]

    half = HEAD_SIZE // 2
    freqs = (theta_base ** (-np.arange(half) * 2.0 / HEAD_SIZE)).astype(np.float32)
    key_table = jax.ShapeDtypeStruct((perms * teams * rows + mine, HEAD_SIZE), jnp.float32)
    query_table = jax.ShapeDtypeStruct((tokens, HEAD_SIZE), jnp.float32)
    key_cos, key_sin, query_cos, query_sin = pl.pallas_call(
        functools.partial(table_kernel, teams, ring, rows, perms),
        name="tab",
        compiler_params=granted(6),
        grid_spec=pltpu.PrefetchScalarGridSpec(
            num_scalar_prefetch=4,
            grid=(1,),
            in_specs=in_vmem(1),
            out_specs=in_vmem(4),
        ),
        out_shape=[key_table, key_table, query_table, query_table],
        cost_estimate=pl.CostEstimate(
            flops=key_table.size * 100, bytes_accessed=key_table.size * 8, transcendentals=0
        ),
    )(pos, lengths, storage_order, orders.reshape(-1), jnp.asarray(np.tile(freqs, 2)[None, :]))

    count = teams * rows + mine
    cost = pl.CostEstimate(
        flops=2 * count * block * teams * HEAD_SIZE,
        bytes_accessed=2 * block * (count + teams * HEAD_SIZE),
        transcendentals=0,
    )
    own_shape = jax.ShapeDtypeStruct((count, HEAD_SIZE), jnp.float32)
    acc_shape = pltpu.VMEM((count, teams * HEAD_SIZE), jnp.float32)
    *key_parts, all_rows = pl.pallas_call(
        functools.partial(key_kernel, teams, ring),
        name="kp",
        compiler_params=granted(14),
        grid_spec=pltpu.PrefetchScalarGridSpec(
            num_scalar_prefetch=1,
            grid=(1,),
            in_specs=in_vmem(teams + 2 * ring),
            out_specs=in_vmem(teams + 1),
            scratch_shapes=[acc_shape],
        ),
        out_shape=[own_shape] * teams + [jax.ShapeDtypeStruct((count, block), jnp.bfloat16)],
        cost_estimate=cost,
    )(pos, chunks[0], *others, *tails, *keys_w)
    key_others = exchanged([part.astype(WIRE) for part in key_parts[1:]])
    value_parts = pl.pallas_call(
        functools.partial(value_kernel, teams, ring),
        name="vp",
        compiler_params=granted(10),
        grid_spec=pltpu.PrefetchScalarGridSpec(
            num_scalar_prefetch=1,
            grid=(1,),
            in_specs=in_vmem(1 + ring),
            out_specs=in_vmem(teams),
            scratch_shapes=[acc_shape],
        ),
        out_shape=[own_shape]
        + [jax.ShapeDtypeStruct(own_shape.shape, jnp.bfloat16)] * (teams - 1),
        cost_estimate=cost,
    )(pos, all_rows, *values_w)
    value_others = exchanged(value_parts[1:])

    def summed(own, others):
        for part in others:
            own = own + part.astype(jnp.float32)
        return own

    key_rows = summed(key_parts[0], key_others)
    turned_keys = pl.pallas_call(
        functools.partial(turn_kernel, perms),
        name="turn",
        compiler_params=granted(6),
        in_specs=in_vmem(3),
        out_specs=pl.BlockSpec(memory_space=pltpu.VMEM),
        out_shape=jax.ShapeDtypeStruct((perms * teams * rows + mine, HEAD_SIZE), jnp.bfloat16),
    )(key_rows, key_cos, key_sin)
    key_pieces = gathered(turned_keys)
    value_rows = summed(value_parts[0], value_others).astype(jnp.bfloat16)
    value_pieces = gathered(value_rows)
    query_others = exchanged([part.astype(WIRE) for part in query_part[1:]])
    query = summed(query_part[0], query_others)

    count = heads * tokens
    attended = pl.pallas_call(
        functools.partial(attend_kernel, perms, ring, teams * rows, tokens),
        name="attend",
        compiler_params=granted(14),
        grid_spec=pltpu.PrefetchScalarGridSpec(
            num_scalar_prefetch=1,
            grid=(1,),
            in_specs=in_vmem(3 + 2 * ring),
            out_specs=pl.BlockSpec(memory_space=pltpu.VMEM),
            scratch_shapes=[
                pltpu.VMEM((tokens, HEAD_SIZE), jnp.bfloat16),
                pltpu.VMEM((tokens, HEAD_SIZE), jnp.bfloat16),
                pltpu.VMEM((count, total_keys), jnp.float32),
            ],
        ),
        out_shape=jax.ShapeDtypeStruct((count, HEAD_SIZE), jnp.bfloat16),
    )(pos, query, query_cos, query_sin, *key_pieces, *value_pieces)

    pieces, bit = {(0, 0): attended}, ring // 2
    ahead = swap(attended, bit)
    for ka, piece in enumerate(exchanged([attended] * (teams - 1))):
        pieces[0, ka + 1] = piece
    for (kb, ka), piece in list(pieces.items()):
        pieces[kb | bit, ka] = ahead if ka == 0 else swap(piece, bit)
    while bit > 1:
        bit //= 2
        for (kb, ka), piece in list(pieces.items()):
            pieces[kb | bit, ka] = swap(piece, bit)

    late = [(kb, ka) for kb, ka in pieces if ka == teams // 2 and kb & (ring // 2)]
    early = [unit for unit in pieces if unit not in late]

    def output(units, before):
        projected_shape = jax.ShapeDtypeStruct((tokens, w_out.shape[1]), jnp.float32)
        shapes = [projected_shape] + [jax.ShapeDtypeStruct((8, tokens), jnp.float32)] * len(before)
        return pl.pallas_call(
            functools.partial(output_kernel, units, teams, ring, tokens, not before),
            compiler_params=granted(10),
            grid_spec=pltpu.PrefetchScalarGridSpec(
                num_scalar_prefetch=1,
                grid=(1,),
                in_specs=in_vmem(len(units) + 1 + len(before)),
                out_specs=in_vmem(len(shapes)),
            ),
            out_shape=shapes,
        )(pos, *[pieces[unit] for unit in units], w_out, *before)

    projected, squares = output(late, output(early, []))
    bit = 1
    while bit < shards:
        squares = squares + swap(squares, bit)
        bit *= 2
    factor = lax.rsqrt(squares[0] / MODEL_WIDTH + epsilon)[:, None]
    return (projected * factor * norm_gain[None, :]).astype(jnp.bfloat16)


def power_of_two(number):
    return number & (number - 1) == 0


def splits(shards, args):
    tail, weight = args[0], args[6]
    teams = weight.shape[1] // HEAD_SIZE
    ring = shards // teams
    return (
        shards % teams == 0
        and power_of_two(shards)
        and power_of_two(teams)
        and ring > 1
        and args[5].shape[1] % (HEAD_SIZE * shards) == 0
        and tail.shape[1] % HEAD_SIZE == 0
        and tail.shape[0] % (16 * ring) == 0
        and power_of_two(tail.shape[0])
        and args[1].shape[0] % 16 == 0
    )


def per_device(*args):
    if splits(lax.axis_size("psg"), args):
        return split_device(*args)
    return general_device(*args)


def solution(mesh):
    placed = (
        P("groups", "psg"),
        P(("groups", "psg"), None),
        P("groups"),
        P("groups"),
        P("groups", None),
        P("psg", None),
        P("psg", None),
        P("psg", None),
        P(None, "psg"),
        P("psg"),
    )
    return jax.shard_map(
        per_device, mesh=mesh, in_specs=placed, out_specs=P("groups", "psg"), check_vma=False
    )
```

```python
import functools

import jax
import jax.numpy as jnp
import numpy as np
from jax import lax
from jax.experimental import pallas as pl
from jax.experimental.pallas import tpu as pltpu
from jax.sharding import PartitionSpec as P


MODEL_WIDTH = 8192
HEAD_SIZE = 128


theta_base = 500000.0
epsilon = 1e-05


def joined(part, axis, combine):
    gathered = jax.tree.map(lambda a: lax.all_gather(a, axis), part)

    def take(source):
        return jax.tree.map(lambda a: lax.dynamic_index_in_dim(a, source, 0, False), gathered)

    return lax.fori_loop(
        1, lax.axis_size(axis), lambda source, state: combine(state, take(source)), take(0)
    )


def rotate(vectors, places):
    half = vectors.shape[-1] // 2
    freqs = theta_base ** (-jnp.arange(half, dtype=jnp.float32) * 2.0 / vectors.shape[-1])
    angles = places.astype(jnp.float32)[:, None] * freqs[None, :]
    cosine = jnp.cos(angles)[:, None, :]
    sine = jnp.sin(angles)[:, None, :]
    first = vectors[..., :half]
    second = vectors[..., half:]
    return jnp.concatenate(
        [first * cosine - second * sine, second * cosine + first * sine], axis=-1
    )


def general_device(
    tail_hidden_states,
    passage_hidden_states,
    lengths,
    storage_order,
    orders,
    w_query,
    key_weight,
    value_weight,
    w_out,
    norm_gain,
):
    shards = lax.axis_size("psg")
    device = lax.axis_index("psg")
    row_count = passage_hidden_states.shape[0]
    tail_count = tail_hidden_states.shape[0]
    kv_heads = key_weight.shape[1] // HEAD_SIZE
    query_heads = w_query.shape[1] // HEAD_SIZE
    query_group = query_heads // kv_heads
    total_keys = row_count * shards
    query_part = jnp.dot(tail_hidden_states, w_query, preferred_element_type=jnp.float32)
    key_part = jnp.dot(tail_hidden_states, key_weight, preferred_element_type=jnp.float32)
    value_part = jnp.dot(tail_hidden_states, value_weight, preferred_element_type=jnp.float32)
    query_sum, key_sum, value_sum = lax.psum((query_part, key_part, value_part), "psg")
    tail_pos = total_keys + jnp.arange(tail_count, dtype=jnp.int32)
    query_vectors = rotate(query_sum.reshape(tail_count, query_heads, HEAD_SIZE), tail_pos).astype(
        jnp.bfloat16
    )
    query_vectors = query_vectors.reshape(tail_count, kv_heads, query_group, HEAD_SIZE)
    tail_key_rows = rotate(key_sum.reshape(tail_count, kv_heads, HEAD_SIZE), tail_pos).astype(
        jnp.bfloat16
    )
    tail_value_rows = value_sum.astype(jnp.bfloat16).reshape(tail_count, kv_heads, HEAD_SIZE)

    def add_block(piece):
        return jnp.dot(passage_hidden_states, piece, preferred_element_type=jnp.float32)

    unrotated_key = add_block(lax.all_gather(key_weight, "psg", axis=0, tiled=True))
    raw_value = add_block(lax.all_gather(value_weight, "psg", axis=0, tiled=True))
    numbers = jnp.arange(lengths.shape[0], dtype=jnp.int32)
    pick = (storage_order[:, None] == numbers[None, :]).astype(jnp.int32)
    stored_lengths = jnp.sum(pick * lengths[None, :], axis=1)
    ends = jnp.cumsum(stored_lengths)
    starts = ends - stored_lengths
    row_ids = device * row_count + jnp.arange(row_count, dtype=jnp.int32)
    slots = jnp.sum((ends[None, :] <= row_ids[:, None]).astype(jnp.int32), axis=1)
    in_slot = (slots[:, None] == numbers[None, :]).astype(jnp.int32)
    offsets = row_ids - jnp.sum(in_slot * starts[None, :], axis=1)
    passage_hot = jnp.dot(in_slot, pick)
    ordered_hot = (orders[:, :, None] == numbers[None, None, :]).astype(jnp.int32)
    ordered_lengths = jnp.sum(ordered_hot * lengths[None, None, :], axis=2)
    order_starts = jnp.cumsum(ordered_lengths, axis=1) - ordered_lengths
    placed = jnp.sum(ordered_hot * order_starts[:, :, None], axis=1)
    token_positions = (
        jnp.sum(passage_hot[None, :, :] * placed[:, None, :], axis=2) + offsets[None, :]
    )
    passage_values = raw_value.astype(jnp.bfloat16).reshape(row_count, kv_heads, HEAD_SIZE)
    unrotated_key = unrotated_key.reshape(row_count, kv_heads, HEAD_SIZE)
    scale = HEAD_SIZE ** (-0.5)
    tail_scores = (
        jnp.einsum(
            "tkgd,skd->tkgs", query_vectors, tail_key_rows, preferred_element_type=jnp.float32
        )
        * scale
    )
    causal = jnp.arange(tail_count)[None, :] <= jnp.arange(tail_count)[:, None]
    tail_scores = jnp.where(causal[:, None, None, :], tail_scores, -1e30)
    tail_top = jnp.max(tail_scores, axis=-1)

    def scores_for(places):
        keys = rotate(unrotated_key, places).astype(jnp.bfloat16)
        return (
            jnp.einsum("tkgd,nkd->tkgn", query_vectors, keys, preferred_element_type=jnp.float32)
            * scale
        )

    def local_stats(places):
        scores = scores_for(places)
        peak = jnp.maximum(jnp.max(scores, axis=-1), tail_top)
        return (peak, jnp.sum(jnp.exp(scores - peak[..., None]), axis=-1))

    def combine(first, second):
        peak = jnp.maximum(first[0], second[0])
        return (peak, first[1] * jnp.exp(first[0] - peak) + second[1] * jnp.exp(second[0] - peak))

    peaks, totals = joined(lax.map(local_stats, token_positions), "psg", combine)

    def accumulate(running, inputs):
        places, peak, partial_value = inputs
        weights = jnp.exp(scores_for(places) - peak[..., None])
        tail_weights = jnp.exp(tail_scores - peak[..., None])
        denom = (partial_value + jnp.sum(tail_weights, axis=-1))[..., None]
        shared = jnp.einsum(
            "tkgn,nkd->tkgd",
            weights.astype(jnp.bfloat16),
            passage_values,
            preferred_element_type=jnp.float32,
        )
        own = jnp.einsum(
            "tkgs,skd->tkgd",
            tail_weights.astype(jnp.bfloat16),
            tail_value_rows,
            preferred_element_type=jnp.float32,
        )
        return ((running[0] + shared / denom, running[1] + own / denom), None)

    start_sums = jnp.zeros((tail_count, kv_heads, query_group, HEAD_SIZE), jnp.float32)
    (shared_sum, own_sum), unused_slot = lax.scan(
        accumulate, (start_sums, start_sums), (token_positions, peaks, totals)
    )
    agreed_output = lax.psum(shared_sum, "psg") + own_sum
    mixed = agreed_output.reshape(tail_count, -1).astype(jnp.bfloat16)
    projected = jnp.dot(mixed, w_out, preferred_element_type=jnp.float32)
    squares = lax.psum(jnp.sum(projected * projected, axis=1), "psg")
    factor = lax.rsqrt(squares / MODEL_WIDTH + epsilon)[:, None]
    return (projected * factor * norm_gain[None, :]).astype(jnp.bfloat16)


WIRE = jnp.float16
ROWS_COLUMNS = (((1,), (1,)), ((), ()))


def granted(mebibytes):
    return pltpu.CompilerParams(vmem_limit_bytes=mebibytes << 20)


def team_at(team, steps, teams):
    return (team + steps) & (teams - 1)


def in_vmem(count):
    return [pl.BlockSpec(memory_space=pltpu.VMEM)] * count


def table_kernel(teams, ring, rows, perms, pos, lengths, storage_order, orders, freq_ref, *out_refs):
    key_cos, key_sin, query_cos, query_sin = out_refs
    passages = lengths.shape[0]
    mine = key_cos.shape[0] - perms * teams * rows
    tokens = mine * ring
    stored = [storage_order[s] for s in range(passages)]
    starts = [jnp.int32(0)]
    for s in range(passages - 1):
        starts.append(starts[-1] + lengths[stored[s]])
    shifts = []
    for r in range(perms):
        first, placed = jnp.int32(0), [jnp.int32(0)] * passages
        for i in range(passages):
            passage = orders[r * passages + i]
            placed = [old + jnp.where(stored[s] == passage, first, 0) for s, old in enumerate(placed)]
            first = first + lengths[passage]
        shifts.append([placed[s] - starts[s] for s in range(passages)])
    lane = lax.broadcasted_iota(jnp.int32, (1, HEAD_SIZE), 1)
    sign = jnp.where(lane < HEAD_SIZE // 2, -1.0, 1.0)

    def write(cos_ref, sin_ref, first, places):
        angles = places.astype(jnp.float32) * freq_ref[...]
        place = slice(first, first + places.shape[0])
        cos_ref[place, :] = jnp.cos(angles)
        sin_ref[place, :] = jnp.sin(angles) * sign

    for ka in range(teams):
        ids = lax.broadcasted_iota(jnp.int32, (rows, HEAD_SIZE), 0) + (ka * ring + pos[1]) * rows
        for r in range(perms):
            shift = shifts[r][0]
            for s in range(1, passages):
                shift = jnp.where(ids >= starts[s], shifts[r][s], shift)
            write(key_cos, key_sin, (r * teams + ka) * rows, ids + shift)
    total = teams * ring * rows
    ids = lax.broadcasted_iota(jnp.int32, (mine, HEAD_SIZE), 0) + (total + pos[1] * mine)
    write(key_cos, key_sin, perms * teams * rows, ids)
    ids = lax.broadcasted_iota(jnp.int32, (tokens, HEAD_SIZE), 0) + total
    write(query_cos, query_sin, 0, ids)


def turned(vectors, cosine, sine):
    return vectors * cosine + pltpu.roll(vectors, HEAD_SIZE // 2, 1) * sine


def bit_order(count):
    width = count.bit_length() - 1
    return [int(format(s, "b").zfill(width)[::-1], 2) if width else 0 for s in range(count)]


def query_kernel(ring, heads, pos, x_ref, w_ref, keep_ref, send_ref, acc_ref):
    acc_ref[...] = jnp.dot(x_ref[...], w_ref[...], preferred_element_type=jnp.float32)
    tokens = x_ref.shape[0]
    for slot, kb in enumerate(bit_order(ring)):
        unit = pos[1] ^ kb
        out = keep_ref if slot < ring // 2 else send_ref
        for j in range(heads):
            column = pl.multiple_of((unit * heads + j) * HEAD_SIZE, HEAD_SIZE)
            out[slot % (ring // 2), 0, j * tokens : (j + 1) * tokens, :] = acc_ref[
                :, pl.ds(column, HEAD_SIZE)
            ]


def project(teams, ring, pos, rows_ref, w_refs, out_refs, acc_ref):
    width = w_refs[0].shape[0]
    total = None
    for kb in range(ring):
        part = jnp.dot(
            rows_ref[:, kb * width : (kb + 1) * width],
            w_refs[kb][...],
            preferred_element_type=jnp.float32,
        )
        total = part if total is None else total + part
    acc_ref[...] = total
    for ka in range(teams):
        column = pl.multiple_of(team_at(pos[0], ka, teams) * HEAD_SIZE, HEAD_SIZE)
        out_refs[ka][...] = acc_ref[:, pl.ds(column, HEAD_SIZE)].astype(out_refs[ka].dtype)


def key_kernel(teams, ring, pos, *refs):
    x_refs, t_refs, w_refs = refs[:teams], refs[teams : teams + ring], refs[teams + ring : teams + 2 * ring]
    *out_refs, all_ref, acc_ref = refs[teams + 2 * ring :]
    rows, width, mine = x_refs[0].shape[0], t_refs[0].shape[1], t_refs[0].shape[0] // ring
    for kb in range(ring):
        column = pl.multiple_of((pos[1] ^ kb) * width, width)
        place = slice(kb * width, (kb + 1) * width)
        for ka in range(teams):
            first = pl.multiple_of(team_at(pos[0], -ka, teams) * rows, rows)
            all_ref[pl.ds(first, rows), place] = x_refs[ka][:, pl.ds(column, width)]
        first = pl.multiple_of(pos[1] * mine, mine)
        all_ref[teams * rows :, place] = t_refs[kb][pl.ds(first, mine), :]
    project(teams, ring, pos, all_ref, w_refs, out_refs, acc_ref)


def value_kernel(teams, ring, pos, rows_ref, *refs):
    project(teams, ring, pos, rows_ref, refs[:ring], refs[ring:-1], refs[-1])


def turn_kernel(perms, k_ref, cos_ref, sin_ref, out_ref):
    rows = (out_ref.shape[0] - k_ref.shape[0]) // (perms - 1)
    for r in range(perms):
        place = slice(r * rows, (r + 1) * rows)
        out_ref[place, :] = turned(k_ref[:rows, :], cos_ref[place, :], sin_ref[place, :]).astype(
            out_ref.dtype
        )
    out_ref[perms * rows :, :] = turned(
        k_ref[rows:, :], cos_ref[perms * rows :, :], sin_ref[perms * rows :, :]
    ).astype(out_ref.dtype)


def attend_kernel(perms, ring, rows, tokens, pos, q_ref, cos_ref, sin_ref, *refs):
    k_refs, v_refs = refs[:ring], refs[ring : 2 * ring]
    out_ref, tk_ref, tv_ref, score_ref = refs[2 * ring :]
    mine = tokens // ring
    base = perms * rows
    scale = HEAD_SIZE ** (-0.5)
    query = jnp.concatenate(
        [
            turned(q_ref[first : first + tokens, :], cos_ref[...], sin_ref[...])
            for first in range(0, q_ref.shape[0], tokens)
        ],
        axis=0,
    ).astype(jnp.bfloat16)
    for kb in range(ring):
        first = pl.multiple_of((pos[1] ^ kb) * mine, mine)
        tk_ref[pl.ds(first, mine), :] = k_refs[kb][base:, :]
        tv_ref[pl.ds(first, mine), :] = v_refs[kb][rows:, :]
    count = q_ref.shape[0]
    tail = (
        lax.dot_general(query, tk_ref[...], ROWS_COLUMNS, preferred_element_type=jnp.float32) * scale
    )
    token = lax.broadcasted_iota(jnp.int32, (count, tokens), 0) & (tokens - 1)
    tail = jnp.where(lax.broadcasted_iota(jnp.int32, (count, tokens), 1) <= token, tail, -1e30)
    tail_top = jnp.max(tail, axis=1, keepdims=True)
    agreed = None
    for r in range(perms):
        top = tail_top
        for kb in range(ring):
            part = (
                lax.dot_general(
                    query,
                    k_refs[kb][r * rows : (r + 1) * rows, :],
                    ROWS_COLUMNS,
                    preferred_element_type=jnp.float32,
                )
                * scale
            )
            score_ref[:, kb * rows : (kb + 1) * rows] = part
            top = jnp.maximum(top, jnp.max(part, axis=1, keepdims=True))
        weights = jnp.exp(tail - top)
        denom = jnp.sum(weights, axis=1, keepdims=True)
        mixed = jnp.dot(
            weights.astype(jnp.bfloat16), tv_ref[...], preferred_element_type=jnp.float32
        )
        for kb in range(ring):
            weights = jnp.exp(score_ref[:, kb * rows : (kb + 1) * rows] - top)
            denom = denom + jnp.sum(weights, axis=1, keepdims=True)
            mixed = mixed + jnp.dot(
                weights.astype(jnp.bfloat16),
                v_refs[kb][:rows, :],
                preferred_element_type=jnp.float32,
            )
        mixed = mixed / denom
        agreed = mixed if agreed is None else agreed + mixed
    out_ref[...] = agreed.astype(out_ref.dtype)


def output_kernel(units, teams, ring, tokens, first_part, pos, *refs):
    y_refs, w_ref, refs = refs[: len(units)], refs[len(units)], refs[len(units) + 1 :]
    heads = y_refs[0].shape[0] // tokens
    total = None if first_part else refs[0][...]
    for (kb, ka), y_ref in zip(units, y_refs, strict=True):
        unit = team_at(pos[0], -ka, teams) * ring + (pos[1] ^ kb)
        first = pl.multiple_of(unit * heads * HEAD_SIZE, HEAD_SIZE)
        left = jnp.concatenate(
            [y_ref[j * tokens : (j + 1) * tokens, :] for j in range(heads)], axis=1
        )
        part = jnp.dot(
            left, w_ref[pl.ds(first, heads * HEAD_SIZE), :], preferred_element_type=jnp.float32
        )
        total = part if total is None else total + part
    if first_part:
        refs[0][...] = total
        return
    refs[1][...] = total
    squares = total * total
    squares = sum(
        squares[:, first : first + HEAD_SIZE] for first in range(0, total.shape[1], HEAD_SIZE)
    )
    sums = jnp.sum(jnp.transpose(squares), axis=0, keepdims=True)
    refs[2][...] = jnp.broadcast_to(sums, refs[2].shape)


def split_device(
    tail_hidden_states,
    passage_hidden_states,
    lengths,
    storage_order,
    orders,
    w_query,
    key_weight,
    value_weight,
    w_out,
    norm_gain,
):
    shards = lax.axis_size("psg")
    device = lax.axis_index("psg")
    teams = key_weight.shape[1] // HEAD_SIZE
    ring = shards // teams
    tokens, width = tail_hidden_states.shape
    rows = passage_hidden_states.shape[0]
    mine = tokens // ring
    team, seat = device // ring, device % ring
    perms = orders.shape[0]
    heads = w_query.shape[1] // (HEAD_SIZE * shards)
    total_keys = rows * shards
    block = width * ring
    pos = jnp.stack([team, seat]).astype(jnp.int32)

    def swap(x, k):
        return lax.ppermute(x, "psg", [(i, i ^ k) for i in range(shards)])

    def gathered(x):
        pieces, bit = {0: x}, ring // 2
        while bit:
            for kb, piece in list(pieces.items()):
                pieces[kb | bit] = swap(piece, bit)
            bit //= 2
        return [pieces[kb] for kb in range(ring)]

    def exchanged(parts):
        moved = []
        for ka, part in enumerate(parts, 1):
            pairs = [(i, (i + ka * ring) % shards) for i in range(shards)]
            moved.append(lax.ppermute(part, "psg", pairs))
        return moved

    chunks = [
        lax.dynamic_slice_in_dim(
            passage_hidden_states, team_at(team, ka, teams) * block, block, 1
        )
        for ka in range(teams)
    ]
    others = exchanged(chunks[1:])
    keys_w = gathered(key_weight)
    tails = gathered(tail_hidden_states)
    values_w = gathered(value_weight)

    units = w_query.shape[1] // teams
    part_shape = jax.ShapeDtypeStruct((ring // 2, teams, heads * tokens, HEAD_SIZE), jnp.float32)
    part_spec = pl.BlockSpec((ring // 2, 1, heads * tokens, HEAD_SIZE), lambda i, pos: (0, i, 0, 0))
    keep, send = pl.pallas_call(
        functools.partial(query_kernel, ring, heads),
        name="qp",
        compiler_params=granted(6),
        grid_spec=pltpu.PrefetchScalarGridSpec(
            num_scalar_prefetch=1,
            grid=(teams,),
            in_specs=[
                pl.BlockSpec((tokens, width), lambda i, pos: (0, 0)),
                pl.BlockSpec((width, units), lambda i, pos: (0, team_at(pos[0], i, teams))),
            ],
            out_specs=[part_spec, part_spec],
            scratch_shapes=[pltpu.VMEM((tokens, units), jnp.float32)],
        ),
        out_shape=[part_shape, part_shape],
        cost_estimate=pl.CostEstimate(
            flops=2 * tokens * width * units * teams,
            bytes_accessed=2 * width * units * teams,
            transcendentals=0,
        ),
    )(pos, tail_hidden_states, pltpu.with_memory_space_constraint(w_query, pltpu.HBM))
    bit = 1
    while True:
        arrived = swap(send, bit)
        query_part = keep + arrived.astype(jnp.float32)
        bit *= 2
        if bit == ring:
            break
        half = query_part.shape[0] // 2
        keep, send = query_part[:half], query_part[half:].astype(WIRE)
    query_part = query_part[0]

    half = HEAD_SIZE // 2
    freqs = (theta_base ** (-np.arange(half) * 2.0 / HEAD_SIZE)).astype(np.float32)
    key_table = jax.ShapeDtypeStruct((perms * teams * rows + mine, HEAD_SIZE), jnp.float32)
    query_table = jax.ShapeDtypeStruct((tokens, HEAD_SIZE), jnp.float32)
    key_cos, key_sin, query_cos, query_sin = pl.pallas_call(
        functools.partial(table_kernel, teams, ring, rows, perms),
        name="tab",
        compiler_params=granted(6),
        grid_spec=pltpu.PrefetchScalarGridSpec(
            num_scalar_prefetch=4,
            grid=(1,),
            in_specs=in_vmem(1),
            out_specs=in_vmem(4),
        ),
        out_shape=[key_table, key_table, query_table, query_table],
        cost_estimate=pl.CostEstimate(
            flops=key_table.size * 100, bytes_accessed=key_table.size * 8, transcendentals=0
        ),
    )(pos, lengths, storage_order, orders.reshape(-1), jnp.asarray(np.tile(freqs, 2)[None, :]))

    count = teams * rows + mine
    cost = pl.CostEstimate(
        flops=2 * count * block * teams * HEAD_SIZE,
        bytes_accessed=2 * block * (count + teams * HEAD_SIZE),
        transcendentals=0,
    )
    own_shape = jax.ShapeDtypeStruct((count, HEAD_SIZE), jnp.float32)
    acc_shape = pltpu.VMEM((count, teams * HEAD_SIZE), jnp.float32)
    *key_parts, all_rows = pl.pallas_call(
        functools.partial(key_kernel, teams, ring),
        name="kp",
        compiler_params=granted(8),
        grid_spec=pltpu.PrefetchScalarGridSpec(
            num_scalar_prefetch=1,
            grid=(1,),
            in_specs=in_vmem(teams + 2 * ring),
            out_specs=in_vmem(teams + 1),
            scratch_shapes=[acc_shape],
        ),
        out_shape=[own_shape] * teams + [jax.ShapeDtypeStruct((count, block), jnp.bfloat16)],
        cost_estimate=cost,
    )(pos, chunks[0], *others, *tails, *keys_w)
    key_others = exchanged([part.astype(WIRE) for part in key_parts[1:]])
    value_parts = pl.pallas_call(
        functools.partial(value_kernel, teams, ring),
        name="vp",
        compiler_params=granted(6),
        grid_spec=pltpu.PrefetchScalarGridSpec(
            num_scalar_prefetch=1,
            grid=(1,),
            in_specs=in_vmem(1 + ring),
            out_specs=in_vmem(teams),
            scratch_shapes=[acc_shape],
        ),
        out_shape=[own_shape]
        + [jax.ShapeDtypeStruct(own_shape.shape, jnp.bfloat16)] * (teams - 1),
        cost_estimate=cost,
    )(pos, all_rows, *values_w)
    value_others = exchanged(value_parts[1:])

    def summed(own, others):
        for part in others:
            own = own + part.astype(jnp.float32)
        return own

    key_rows = summed(key_parts[0], key_others)
    turned_keys = pl.pallas_call(
        functools.partial(turn_kernel, perms),
        name="turn",
        compiler_params=granted(6),
        in_specs=in_vmem(3),
        out_specs=pl.BlockSpec(memory_space=pltpu.VMEM),
        out_shape=jax.ShapeDtypeStruct((perms * teams * rows + mine, HEAD_SIZE), jnp.bfloat16),
    )(key_rows, key_cos, key_sin)
    key_pieces = gathered(turned_keys)
    value_rows = summed(value_parts[0], value_others).astype(jnp.bfloat16)
    value_pieces = gathered(value_rows)
    query_others = exchanged([part.astype(WIRE) for part in query_part[1:]])
    query = summed(query_part[0], query_others)

    count = heads * tokens
    attended = pl.pallas_call(
        functools.partial(attend_kernel, perms, ring, teams * rows, tokens),
        name="attend",
        compiler_params=granted(8),
        grid_spec=pltpu.PrefetchScalarGridSpec(
            num_scalar_prefetch=1,
            grid=(1,),
            in_specs=in_vmem(3 + 2 * ring),
            out_specs=pl.BlockSpec(memory_space=pltpu.VMEM),
            scratch_shapes=[
                pltpu.VMEM((tokens, HEAD_SIZE), jnp.bfloat16),
                pltpu.VMEM((tokens, HEAD_SIZE), jnp.bfloat16),
                pltpu.VMEM((count, total_keys), jnp.float32),
            ],
        ),
        out_shape=jax.ShapeDtypeStruct((count, HEAD_SIZE), jnp.bfloat16),
    )(pos, query, query_cos, query_sin, *key_pieces, *value_pieces)

    pieces, bit = {(0, 0): attended}, ring // 2
    ahead = swap(attended, bit)
    for ka, piece in enumerate(exchanged([attended] * (teams - 1))):
        pieces[0, ka + 1] = piece
    for (kb, ka), piece in list(pieces.items()):
        pieces[kb | bit, ka] = ahead if ka == 0 else swap(piece, bit)
    while bit > 1:
        bit //= 2
        for (kb, ka), piece in list(pieces.items()):
            pieces[kb | bit, ka] = swap(piece, bit)

    late = [(kb, ka) for kb, ka in pieces if ka == teams // 2 or ka and kb & (ring // 2)]
    early = [unit for unit in pieces if unit not in late]

    def output(units, before):
        projected_shape = jax.ShapeDtypeStruct((tokens, w_out.shape[1]), jnp.float32)
        shapes = [projected_shape] + [jax.ShapeDtypeStruct((8, tokens), jnp.float32)] * len(before)
        return pl.pallas_call(
            functools.partial(output_kernel, units, teams, ring, tokens, not before),
            compiler_params=granted(6),
            grid_spec=pltpu.PrefetchScalarGridSpec(
                num_scalar_prefetch=1,
                grid=(1,),
                in_specs=in_vmem(len(units) + 1 + len(before)),
                out_specs=in_vmem(len(shapes)),
            ),
            out_shape=shapes,
        )(pos, *[pieces[unit] for unit in units], w_out, *before)

    projected, squares = output(late, output(early, []))
    bit = 1
    while bit < shards:
        squares = squares + swap(squares, bit)
        bit *= 2
    factor = lax.rsqrt(squares[0] / MODEL_WIDTH + epsilon)[:, None]
    return (projected * factor * norm_gain[None, :]).astype(jnp.bfloat16)


def power_of_two(number):
    return number & (number - 1) == 0


def splits(shards, args):
    tail, weight = args[0], args[6]
    teams = weight.shape[1] // HEAD_SIZE
    ring = shards // teams
    return (
        shards % teams == 0
        and power_of_two(shards)
        and power_of_two(teams)
        and ring > 1
        and args[5].shape[1] % (HEAD_SIZE * shards) == 0
        and tail.shape[1] % HEAD_SIZE == 0
        and tail.shape[0] % (16 * ring) == 0
        and power_of_two(tail.shape[0])
        and args[1].shape[0] % 16 == 0
    )


def per_device(*args):
    if splits(lax.axis_size("psg"), args):
        return split_device(*args)
    return general_device(*args)


def solution(mesh):
    placed = (
        P("groups", "psg"),
        P(("groups", "psg"), None),
        P("groups"),
        P("groups"),
        P("groups", None),
        P("psg", None),
        P("psg", None),
        P("psg", None),
        P(None, "psg"),
        P("psg"),
    )
    return jax.shard_map(
        per_device, mesh=mesh, in_specs=placed, out_specs=P("groups", "psg"), check_vma=False
    )
```
